32 devices in a mesh: cand: 2 (over y), gx: 4 (over z), gy: 2 (over x), ha: 2 (over core).
Axes of the slice: x: 2, y: 2, z: 4, core: 2. Of those that a mesh axis runs over, the one named last changes fastest.
Arguments:
- forward_field: float32 [4, 2, 3, 32, 16, 256], P('ha', None, None, ('cand', 'gx'), 'gy'), parts along dimension 3, may hold values from -4 to 4
- adjoint_source: float32 [4, 2, 3, 32, 16, 256], P('ha', None, None, ('cand', 'gx'), 'gy'), parts along dimension 3, may hold values from -60 to 60
- permittivity: float32 [32, 16, 256], P(('cand', 'gx'), 'gy'), parts along dimension 0, may hold values from 1 to 12
- frequency: float32 [4], replicated, may hold values from 0.1 to 0.35
- design_tiles: int32 [8, 4], P(('cand', 'gx'), 'gy'), parts along dimension 0, may hold values from 0 to 1, as said below
- mix_pairs: int32 [4, 3, 2], replicated, may hold values from 0 to 3
- pml_width: int32 [3], replicated, may hold values from 2 to 5
Outputs:
- adjoint_field: float32 [4, 2, 3, 32, 16, 256], P('ha', None, None, ('cand', 'gx'), 'gy'), parts along dimension 3
- gradient: float32 [32, 16, 256], P(('cand', 'gx'), 'gy'), parts along dimension 0
The draws below stay inside these ranges and needn't reach their ends.
There are 2 independent parts, one for each index of `cand`. The reference program is written for one: setup_inputs(seed, part) draws one part's arguments, and reference() takes and returns one part's arrays. A program takes and returns all parts, laid end to end along the dimension named above; an argument that names none is the same for every part. Nothing has to cross between parts.
Inputs may be any that keep to these rules, and one draw needn't show every extreme that they name: `design_tiles`: 1 marks a design tile of 4 x 4 columns of cells; all ones lie in one rectangle of tiles that spans 1 to 3 devices' widths along x and 1 to 2 along y, and at least one tile is 1. `mix_pairs`: entries name harmonics.
All inputs are finite; a program needn't handle non-finite values.
Results may differ from the reference program's by a relative error of at most 0.0001.
Values sent between devices are 32-bit elements; how exact they have to be, the bound alone decides.
A program may use at most 64 MiB of HBM per device.

```python
import math
import jax
import jax.numpy as jnp
from jax import lax

HARMONICS = 4
PAIRS = 3
ITERS = 3
TILE = 4
CX = 4
CY = 8
NX = 16
NY = 16
NZ = 256


def draw_design_tiles(key, part):
    key_a, key_b, key_c, key_d, key_e = jax.random.split(jax.random.fold_in(key, 17), 5)
    rows = NX // TILE
    cols = NY // TILE
    span_x = jax.random.randint(key_a, (), CX // TILE, 3 * CX // TILE + 1)
    span_y = jax.random.randint(key_b, (), CY // TILE, 2 * CY // TILE + 1)
    start_x = jax.random.randint(key_c, (), 0, rows - span_x + 1)
    start_y = jax.random.randint(key_d, (), 0, cols - span_y + 1)
    index_x = jnp.arange(rows)[:, None]
    index_y = jnp.arange(cols)[None, :]
    inside = (index_x >= start_x) & (index_x < start_x + span_x) & (index_y >= start_y) & (index_y < start_y + span_y)
    corner = (index_x == start_x) & (index_y == start_y)
    filled = (jax.random.randint(key_e, (rows, cols), 0, 4) > 0) | corner
    return (inside & filled).astype(jnp.int32)


def touch_ends(drawn, own_key, low, top_value):
    extent = drawn.shape
    spot = [jax.random.randint(jax.random.fold_in(own_key, axis), (), 0, extent[axis]) for axis in range(len(extent))]
    drawn = drawn.at[tuple(spot)].set(low)
    longest = extent.index(max(extent))
    spot[longest] = (spot[longest] + 1) % extent[longest]
    return drawn.at[tuple(spot)].set(top_value)


def levels(key, shape, cuts, low, largest):
    factor_of = 1.0
    for axis_at, shards_of in cuts:
        draws = jax.random.uniform(jax.random.fold_in(jax.random.fold_in(key, 6), axis_at), (shards_of,), jnp.float32, low / len(cuts), largest / len(cuts))
        factor_of = factor_of * jnp.repeat(jnp.exp(draws), shape[axis_at] // shards_of).reshape((-1,) + (1,) * (len(shape) - 1 - axis_at))
    return factor_of


def centred(rng, dims, deviation, most, cuts=(), kind=jnp.bfloat16):
    array = deviation * jax.random.normal(rng, dims, jnp.float32)
    if cuts:
        array = array * levels(rng, dims, cuts, -0.22, 0.18)
    return jnp.clip(array, -most, most).astype(kind)


def setup_inputs(seed: int = 0, part: int = 0) -> dict:
    keys = jax.random.split(jax.random.key(seed), 8)
    part_splits = jax.random.split(jax.random.fold_in(keys[7], part), 8)
    forward_field = centred(part_splits[0], (HARMONICS, 2, 3, NX, NY, NZ), 1.0, 4.0, ((0, 2), (3, 4), (4, 2)), jnp.float32)
    adjoint_source = centred(part_splits[1], (HARMONICS, 2, 3, NX, NY, NZ), 10.0, 60.0, ((0, 2), (3, 4), (4, 2)), jnp.float32)
    permittivity = jnp.clip(1.0 + 11.0 * jax.random.uniform(part_splits[2], (NX, NY, NZ), jnp.float32) ** levels(part_splits[2], (NX, NY, NZ), ((0, 4), (1, 2)), -0.2, 0.2), 1.0, 12.0)
    frequency = jnp.clip(jnp.exp(jax.random.uniform(keys[3], (HARMONICS,), jnp.float32, math.log(0.1), math.log(0.35))), 0.1, 0.35)
    design_tiles = draw_design_tiles(jax.random.fold_in(jax.random.fold_in(keys[7], part), 71), part)
    mix_pairs = touch_ends(jax.random.randint(keys[5], (HARMONICS, PAIRS, 2), 0, HARMONICS), jax.random.fold_in(keys[5], 1), 0, HARMONICS - 1).astype(jnp.int32)
    pml_width = jax.random.randint(keys[6], (3,), 2, 6).astype(jnp.int32)
    return {"forward_field": forward_field, "adjoint_source": adjoint_source, "permittivity": permittivity, "frequency": frequency, "design_tiles": design_tiles, "mix_pairs": mix_pairs, "pml_width": pml_width}


kerr_coef = 4.0
sigma_peak = 8.0


def zero_rim(values, along):
    return jnp.zeros_like(lax.slice_in_dim(values, 0, 1, axis=along))


def step_ahead(values, upcoming, along):
    rest = lax.slice_in_dim(values, 1, values.shape[along], axis=along)
    return jnp.concatenate([rest, upcoming], axis=along) - values


def step_behind(values, earlier, along):
    rest = lax.slice_in_dim(values, 0, values.shape[along] - 1, axis=along)
    return values - jnp.concatenate([earlier, rest], axis=along)


def curl_ahead(field_x, field_y, field_z, ahead_x, ahead_y, ahead_z):
    first = field_x.ndim - 3
    second = first + 1
    third = first + 2
    mag_x = step_ahead(field_z, ahead_y[1], second) - step_ahead(field_y, ahead_z[1], third)
    mag_y = step_ahead(field_x, ahead_z[0], third) - step_ahead(field_z, ahead_x[1], first)
    mag_z = step_ahead(field_y, ahead_x[0], first) - step_ahead(field_x, ahead_y[0], second)
    return mag_x, mag_y, mag_z


def curl_behind(mag_x, mag_y, mag_z, behind_x, behind_y, behind_z):
    first = mag_x.ndim - 3
    second = first + 1
    third = first + 2
    out_x = step_behind(mag_z, behind_y[1], second) - step_behind(mag_y, behind_z[1], third)
    out_y = step_behind(mag_x, behind_z[0], third) - step_behind(mag_z, behind_x[1], first)
    out_z = step_behind(mag_y, behind_x[0], first) - step_behind(mag_x, behind_y[0], second)
    return out_x, out_y, out_z


def plain_curl(adjoint):
    field_x = adjoint[:, :, 0]
    field_y = adjoint[:, :, 1]
    field_z = adjoint[:, :, 2]
    first = field_x.ndim - 3
    rim_x = zero_rim(field_x, first)
    rim_y = zero_rim(field_x, first + 1)
    rim_z = zero_rim(field_x, first + 2)
    mag_x, mag_y, mag_z = curl_ahead(field_x, field_y, field_z, (rim_x, rim_x), (rim_y, rim_y), (rim_z, rim_z))
    out_x, out_y, out_z = curl_behind(mag_x, mag_y, mag_z, (rim_x, rim_x), (rim_y, rim_y), (rim_z, rim_z))
    return jnp.stack([out_x, out_y, out_z], axis=2)


def complex_pairs(chosen_field, chosen_adjoint):
    real = jnp.sum(chosen_field[:, :, 0] * chosen_adjoint[:, :, 0] - chosen_field[:, :, 1] * chosen_adjoint[:, :, 1], axis=1)
    imag = jnp.sum(chosen_field[:, :, 0] * chosen_adjoint[:, :, 1] + chosen_field[:, :, 1] * chosen_adjoint[:, :, 0], axis=1)
    return jnp.stack([real, imag], axis=1)


def absorb_profile(width, count, offset, length):
    place = offset + jnp.arange(length, dtype=jnp.int32)
    reach = jnp.maximum(jnp.maximum(width - place, place - (count - 1 - width)), 0)
    return (reach.astype(jnp.float32) / width.astype(jnp.float32)) ** 2


def tiles_to_cells(tiles, tile):
    rows, cols = tiles.shape
    spread = jnp.broadcast_to(tiles[:, None, :, None], (rows, tile, cols, tile))
    return spread.reshape(rows * tile, cols * tile).astype(jnp.float32)[:, :, None]


def reference(forward_field, adjoint_source, permittivity, frequency, design_tiles, mix_pairs, pml_width):
    mask = tiles_to_cells(design_tiles, TILE)
    anchor = jnp.zeros((), jnp.int32)
    sigma = sigma_peak * (absorb_profile(pml_width[0], NX, anchor, NX)[:, None, None]
                          + absorb_profile(pml_width[1], NY, anchor, NY)[None, :, None]
                          + absorb_profile(pml_width[2], NZ, anchor, NZ)[None, None, :])
    squared = frequency * frequency
    weight = squared[:, None, None, None, None, None]
    scale = 10.0 + weight * permittivity
    chosen_field = forward_field[mix_pairs[:, :, 0]]
    adjoint = adjoint_source / scale
    for sweep in range(ITERS):
        chosen_adjoint = adjoint[mix_pairs[:, :, 1]]
        kerr = complex_pairs(chosen_field, chosen_adjoint)
        turned = jnp.stack([-adjoint[:, 1], adjoint[:, 0]], axis=1)
        applied = plain_curl(adjoint) - weight * (permittivity * adjoint + sigma * turned + kerr_coef * mask * kerr)
        adjoint = adjoint + (adjoint_source - applied) / scale
    product = adjoint[:, 0] * forward_field[:, 0] - adjoint[:, 1] * forward_field[:, 1]
    gradient = mask * jnp.sum(squared[:, None, None, None, None] * product, axis=(0, 1))
    return adjoint, gradient
```

```python
import functools

import jax
import jax.numpy as jnp
from jax import lax
from jax.experimental import pallas as pl
from jax.experimental.pallas import tpu as pltpu
from jax.sharding import PartitionSpec as P

ITERS = 3
TILE = 4
PAIRS = 3

kerr_coef = 4.0
sigma_peak = 8.0

MESH = pl.DeviceIdType.MESH
XUP, XDN, YUP, YDN, CUP, CDN, HA = range(7)
YUP2, YDN2 = 12, 13
GRAIN = (2, 2, 2)


def cut(own, s):
    cells = [(h, p) for h in range(own) for p in range(2)]
    size = {4: 1, 2: 2, 1: 2 * own}[GRAIN[s]]
    return [cells[i : i + size] for i in range(0, 2 * own, size)]


def recv_slots(own):
    messages = [
        (kind, s, u)
        for s in range(ITERS)
        for u in range(len(cut(own, s)))
        for kind in range(7)
    ]
    messages += [(kind, 1, u) for u in range(len(cut(own, 1))) for kind in (YUP2, YDN2)]
    return {message: at for at, message in enumerate(messages)}


def kernel(
    size_x,
    size_y,
    fwd,
    src_hbm,
    perm_hbm,
    freq_hbm,
    tiles_hbm,
    mix_hbm,
    pml_hbm,
    out,
    gout,
    freq,
    tiles,
    mix,
    pml,
    fall,
    v0,
    v1,
    v2,
    src,
    perm,
    inv,
    gain,
    loss,
    kmask,
    held,
    part,
    other,
    xup_s,
    xup_r,
    xdn_r,
    yup_s,
    yup_r,
    ydn_s,
    ydn_r,
    cup_s,
    cup_r,
    cdn_s,
    cdn_r,
    load_sem,
    send_sem,
    recv_sem,
    fwd_sem,
    grad_sem,
    scalar_sem,
):
    own, _, _, cx, cy, cz = src.shape
    vs = (v0, v1, v2)
    gx = lax.axis_index("gx")
    gy = lax.axis_index("gy")
    ha = lax.axis_index("ha")
    has_xm, has_xp = gx > 0, gx < size_x - 1
    has_ym, has_yp = gy > 0, gy < size_y - 1
    xm, xp = jnp.maximum(gx - 1, 0), jnp.minimum(gx + 1, size_x - 1)
    ym, yp = jnp.maximum(gy - 1, 0), jnp.minimum(gy + 1, size_y - 1)
    mate = {"ha": 1 - ha}
    mine, theirs = ha * own, (1 - ha) * own
    made = (mine, mine, theirs)
    work = (mine, theirs, mine)

    load_scalars = [
        pltpu.make_async_copy(source, target, scalar_sem.at[i])
        for i, (source, target) in enumerate(
            ((freq_hbm, freq), (pml_hbm, pml), (tiles_hbm, tiles), (mix_hbm, mix))
        )
    ]
    load_perm = pltpu.make_async_copy(perm_hbm, perm, load_sem.at[0])
    load_src = [
        pltpu.make_async_copy(src_hbm.at[h], src.at[h], load_sem.at[1 + h]) for h in range(own)
    ]
    load_fwd = pltpu.make_async_copy(fwd, fall.at[pl.ds(mine, own)], load_sem.at[1 + own])
    load_scalars[0].start()
    load_perm.start()
    for copy in load_src:
        copy.start()

    barrier = pltpu.get_barrier_semaphore()
    peers = (
        (has_xp, {"gx": xp}),
        (has_xm, {"gx": xm}),
        (has_yp, {"gy": yp}),
        (has_ym, {"gy": ym}),
        (has_xp & has_ym, {"gx": xp, "gy": ym}),
        (has_xm & has_yp, {"gx": xm, "gy": yp}),
    )
    pl.semaphore_signal(barrier, inc=1, device_id=mate, device_id_type=MESH)
    count = jnp.int32(1)
    for there, peer in peers:
        count = count + 2 * there.astype(jnp.int32)

        @pl.when(there)
        def _():
            for core in (ha, 1 - ha):
                pl.semaphore_signal(
                    barrier, inc=1, device_id=peer | {"ha": core}, device_id_type=MESH
                )

    for copy in load_scalars[1:]:
        copy.start()
    load_fwd.start()

    units = [cut(own, s) for s in range(ITERS)]
    slots = recv_slots(own)
    half = cx // 2
    every, low, high = pl.ds(0, cx), pl.ds(0, half), pl.ds(half, cx - half)
    low_up, high_up = pl.ds(0, half - 1), pl.ds(half - 1, cx - half + 1)

    def which(s, u, base=0):
        h, p = units[s][u][0]
        kind = GRAIN[s]
        if kind == 4:
            return base + h, p
        return (base + h, slice(None)) if kind == 2 else (pl.ds(base, own), slice(None))

    def spot(ref, s, u, rows=None):
        return ref.at[(s,) + which(s, u) + (() if rows is None else (rows,))]

    def block(v, s, base, u, tail):
        return v.at[which(s, u, base) + tail]

    def link(kind, s, u):
        v = vs[s]
        to = {} if s == 0 else mate
        parted = s == 1
        first_up, first = (low_up, low) if parted else (every, every)
        if kind == HA:
            source = target = block(v, s, made[s], u, (slice(None),))
            peer, sends, gets = mate, None, None
        else:
            face, halo, rows, peer, sends, gets = {
                XUP: (xup_s, xup_r, None, {"gx": xp}, has_xp, has_xm),
                XDN: (None, xdn_r, None, {"gx": xm}, has_xm, has_xp),
                YUP: (yup_s, yup_r, first_up, {"gy": yp}, has_yp, has_ym),
                YDN: (ydn_s, ydn_r, first, {"gy": ym}, has_ym, has_yp),
                YUP2: (yup_s, yup_r, high_up, {"gy": yp}, has_yp, has_ym),
                YDN2: (ydn_s, ydn_r, high, {"gy": ym}, has_ym, has_yp),
                CUP: (cup_s, cup_r, None, {"gx": xp, "gy": ym}, has_xp & has_ym, has_xm & has_yp),
                CDN: (cdn_s, cdn_r, None, {"gx": xm, "gy": yp}, has_xm & has_yp, has_xp & has_ym),
            }[kind]
            peer = peer | to
            target = spot(halo, s, u, rows)
            if kind == XDN:
                source = block(v, s, made[s], u, (pl.ds(1, 2), 0))
            else:
                source = spot(face, s, u, rows)
        copy = pltpu.make_async_remote_copy(
            src_ref=source,
            dst_ref=target,
            send_sem=send_sem.at[HA + s if kind == HA else kind % 10],
            recv_sem=recv_sem.at[slots[kind, s, u]],
            device_id=peer,
            device_id_type=MESH,
        )
        return copy, sends, gets

    def send(kind, s, u):
        copy, sends, _ = link(kind, s, u)
        if sends is None:
            copy.start()
        else:
            pl.when(sends)(copy.start)

    def all_sent():
        for kind, halo in enumerate((xup_r, xdn_r, yup_r, ydn_r, cup_r, cdn_r)):
            copy, sends, _ = link(kind, 0, 0)
            total = pltpu.make_async_remote_copy(
                src_ref=halo,
                dst_ref=halo,
                send_sem=send_sem.at[kind],
                recv_sem=recv_sem.at[0],
                device_id=mate,
                device_id_type=MESH,
            )
            pl.when(sends)(total.wait_send)
        for s in range(ITERS):
            total = vs[s].at[pl.ds(made[s], own)]
            pltpu.make_async_remote_copy(
                src_ref=total,
                dst_ref=total,
                send_sem=send_sem.at[HA + s],
                recv_sem=recv_sem.at[0],
                device_id=mate,
                device_id_type=MESH,
            ).wait_send()

    def arrived(kind, s, u):
        if kind == HA:
            place = block(vs[s], s, own - made[s], u, (slice(None),))
            pltpu.make_async_remote_copy(
                src_ref=place,
                dst_ref=place,
                send_sem=send_sem.at[HA + s],
                recv_sem=recv_sem.at[slots[kind, s, u]],
                device_id=mate,
                device_id_type=MESH,
            ).wait_recv()
        else:
            copy, _, gets = link(kind, s, u)
            pl.when(gets)(copy.wait_recv)

    iy = lax.broadcasted_iota(jnp.int32, (cy, cz), 0)
    iz = lax.broadcasted_iota(jnp.int32, (cy, cz), 1)
    keep_x = has_xm.astype(jnp.float32)
    keep_y = has_ym.astype(jnp.float32)

    def z_ahead(f):
        return jnp.where(iz == cz - 1, 0.0, pltpu.roll(f, cz - 1, 1))

    def z_behind(f):
        return jnp.where(iz == 0, 0.0, pltpu.roll(f, 1, 1))

    def y_ahead(f, row):
        return jnp.where(iy == cy - 1, row, pltpu.roll(f, cy - 1, 0))

    def y_behind(f, row):
        return jnp.where(iy == 0, row, pltpu.roll(f, 1, 0))

    def profile(width, extent, place):
        reach = jnp.maximum(jnp.maximum(width - place, place - (extent - 1 - width)), 0)
        ratio = reach.astype(jnp.float32) / jnp.full((cy, cz), width).astype(jnp.float32)
        return ratio * ratio

    def pack_up(s, h, p, f):
        fx, fy, fz = (f(c, cx - 1) for c in range(3))
        cup_s[s, h, p] = fx[0:1]
        xup_s[s, h, p, 0] = fy + y_ahead(fx, 0.0) - fx
        xup_s[s, h, p, 1] = fz + z_ahead(fx) - fx

    def pack_down(s, h, p, f):
        cdn_s[s, h, p] = f(1, 0)[cy - 1 : cy]

    def pack_y(s, h, p, f, up, down):
        for x in up:
            fx, fy, fz = (f(c, x)[cy - 1 : cy] for c in range(3))
            ahead = f(1, x + 1)[cy - 1 : cy] if x < cx - 1 else 0.0
            row_z = jnp.where(iz[0:1] == cz - 1, 0.0, pltpu.roll(fy, cz - 1, 1))
            yup_s[s, h, p, x, 0:1, :] = fx + ahead - fy
            yup_s[s, h, p, x, 1:2, :] = fz + row_z - fy
        for x in down:
            ydn_s[s, h, p, x, 0:1, :] = f(0, x)[0:1]
            ydn_s[s, h, p, x, 1:2, :] = f(2, x)[0:1]

    def send_all(s, kinds, u):
        for kind in kinds:
            send(kind, s, u)

    load_scalars[0].wait()
    squared = [freq[i] * freq[i] for i in range(2 * own)]
    squared_mine = [freq[mine + h] * freq[mine + h] for h in range(own)]
    load_perm.wait()
    scales = {}
    for h in range(own):
        for x in range(cx):
            scales[h, x] = 1.0 / (10.0 + squared_mine[h] * perm[x])
    for h in range(own):
        load_src[h].wait()
        for p in range(2):
            f = {}
            for x in range(cx):
                for c in range(3):
                    f[c, x] = src[h, p, c, x] * scales[h, x]
                    v0[mine + h, p, c, x] = f[c, x]
            take = lambda c, x: f[c, x]
            pack_up(0, h, p, take)
            pack_down(0, h, p, take)
            pack_y(0, h, p, take, range(cx), range(cx))

    pl.semaphore_wait(barrier, count)
    for u in range(len(units[0])):
        send_all(0, (CUP, CDN, XUP, XDN, YUP, YDN, HA), u)
    fwd_copy = pltpu.make_async_remote_copy(
        src_ref=fwd,
        dst_ref=fall.at[pl.ds(mine, own)],
        send_sem=fwd_sem.at[0],
        recv_sem=fwd_sem.at[1],
        device_id=mate,
        device_id_type=MESH,
    )
    fwd_copy.start()

    for there, halo in (
        (has_xm, xup_r),
        (has_xp, xdn_r),
        (has_ym, yup_r),
        (has_yp, ydn_r),
        (has_xm & has_yp, cup_r),
        (has_xp & has_ym, cdn_r),
    ):

        @pl.when(jnp.logical_not(there))
        def _():
            halo[...] = jnp.zeros_like(halo)

    for copy in load_scalars[1:]:
        copy.wait()
    sigma_yz = profile(pml[1], cy * size_y, gy * cy + iy) + profile(pml[2], cz, iz)
    masks = []
    for x in range(cx):
        place = jnp.full((cy, cz), gx * cx + x)
        sigma = sigma_peak * (profile(pml[0], cx * size_x, place) + sigma_yz)
        mask = jnp.zeros((cy, cz), jnp.float32)
        for t in range(cy // TILE):
            inside = (iy >= t * TILE) & (iy < (t + 1) * TILE)
            mask = jnp.where(inside, tiles[x // TILE, t].astype(jnp.float32), mask)
        for i in range(2 * own):
            weighed = squared[i] * perm[x]
            inv[i, x] = 1.0 / (10.0 + weighed)
            gain[i, x] = 10.0 + 2.0 * weighed
            loss[i, x] = squared[i] * sigma
            kmask[i, x] = (kerr_coef * squared[i]) * mask
        masks.append(mask)

    def fwd_arrived():
        load_fwd.wait()
        pltpu.make_async_remote_copy(
            src_ref=fwd,
            dst_ref=fall.at[pl.ds(theirs, own)],
            send_sem=fwd_sem.at[0],
            recv_sem=fwd_sem.at[1],
            device_id=mate,
            device_id_type=MESH,
        ).wait_recv()

    grads = {}

    def local(s, planes):
        v = vs[s]
        base = work[s]
        for h in range(own):
            gh = base + h
            for p in range(2):
                field = lambda c, x: v[gh, p, c, x]
                mz_behind = my_behind = None
                for x in planes:
                    fx, fy, fz = field(0, x), field(1, x), field(2, x)
                    fy_ahead = field(1, x + 1) if x < cx - 1 else 0.0
                    fz_ahead = field(2, x + 1) if x < cx - 1 else 0.0
                    mx = (y_ahead(fz, 0.0) - fz) - (z_ahead(fy) - fy)
                    my = (z_ahead(fx) - fx) - (fz_ahead - fz)
                    mz = (fy_ahead - fy) - (y_ahead(fx, 0.0) - fx)
                    if x == 0:
                        mz_behind, my_behind = keep_x * fy, -keep_x * fz
                    elif mz_behind is None:
                        bx, by, bz = (field(c, x - 1) for c in range(3))
                        my_behind = (z_ahead(bx) - bx) - (fz - bz)
                        mz_behind = (fy - by) - (y_ahead(bx, 0.0) - bx)
                    mz_low = y_behind(mz, -keep_y * fx)
                    mx_low = y_behind(mx, keep_y * fz)
                    curls = (
                        (mz - mz_low) - (my - z_behind(my)),
                        (mx - z_behind(mx)) - (mz - mz_behind),
                        (my - my_behind) - (mx - mx_low),
                    )
                    my_behind, mz_behind = my, mz
                    k1, k2 = gain[gh, x], loss[gh, x]
                    scale = 0.5 * k1 + 5.0
                    for c, at_c in enumerate((fx, fy, fz)):
                        turned = k2 * v[gh, 1 - p, c, x]
                        turned = -turned if p == 0 else turned
                        given = src[h, p, c, x] if s != 1 else v0[gh, p, c, x] * scale
                        held[h, p, c, x] = given + k1 * at_c + turned - curls[c]

    def mixed(s, planes):
        v = vs[s]
        base = work[s]
        for h in range(own):
            firsts = [mix[k, 0, base + h] for k in range(PAIRS)]
            seconds = [mix[k, 1, base + h] for k in range(PAIRS)]
            for x in planes:
                k3 = kmask[base + h, x]
                for c in range(3):
                    real = imag = None
                    for a, b in zip(firsts, seconds):
                        fr, fi = fall[a, 0, c, x], fall[a, 1, c, x]
                        vr, vi = v[b, 0, c, x], v[b, 1, c, x]
                        re, im = fr * vr - fi * vi, fr * vi + fi * vr
                        real = re if real is None else real + re
                        imag = im if imag is None else imag + im
                    held[h, 0, c, x] = held[h, 0, c, x] + k3 * real
                    held[h, 1, c, x] = held[h, 1, c, x] + k3 * imag

    def finish(s, h, p, planes):
        gh = work[s] + h
        f = {}
        for x in planes:
            scale = inv[gh, x]
            row = lambda ref, c, at: ref[s, h, p, at, c : c + 1, :]
            fx_next, fz_next = row(ydn_r, 0, x), row(ydn_r, 1, x)
            low_z, low_x = row(yup_r, 0, x), row(yup_r, 1, x)
            if x == cx - 1:
                low_z = low_z + cdn_r[s, h, p]
            fx_prev = row(ydn_r, 0, x - 1) if x > 0 else cup_r[s, h, p]
            fz_step = fz_next - jnp.where(iz[0:1] == 0, 0.0, pltpu.roll(fz_next, 1, 1))
            less_x = jnp.where(iy == 0, low_z, jnp.where(iy == cy - 1, fx_next, 0.0))
            less_y = jnp.where(iy == cy - 1, fx_prev - fx_next - fz_step, 0.0)
            less_z = jnp.where(iy == 0, low_x, jnp.where(iy == cy - 1, fz_next, 0.0))
            if x == 0:
                less_y = less_y + xup_r[s, h, p, 0]
                less_z = less_z + xup_r[s, h, p, 1]
            if x == cx - 1:
                fy_ahead, fz_ahead = xdn_r[s, h, p, 0], xdn_r[s, h, p, 1]
                steps = (fy_ahead - y_behind(fy_ahead, 0.0)) + (fz_ahead - z_behind(fz_ahead))
                less_x = less_x - steps
                less_y = less_y + fy_ahead
                less_z = less_z + fz_ahead
            total = None
            for c, less in enumerate((less_x, less_y, less_z)):
                new = scale * (held[h, p, c, x] + less)
                f[c, x] = new
                if s < ITERS - 1:
                    vs[s + 1][gh, p, c, x] = new
                else:
                    out[h, p, c, x] = new
                    term = new * fall[gh, p, c, x]
                    total = term if total is None else total + term
            if s == ITERS - 1:
                total = (squared_mine[h] if p == 0 else -squared_mine[h]) * total
                grads[x] = grads[x] + total if x in grads else total
        if s == ITERS - 1:
            return None
        v = vs[s + 1]
        return lambda c, x: f[c, x] if (c, x) in f else v[gh, p, c, x]

    def stage(s, waits, planes, packs, sends):
        pending = [(kind, u) for u in range(len(units[s])) for kind in waits]
        for v, unit in enumerate(units[s + 1] if s < ITERS - 1 else units[s]):
            for kind, u in list(pending):
                if set(units[s][u]) & set(unit):
                    arrived(kind, s, u)
                    pending.remove((kind, u))
            for h, p in unit:
                f = finish(s, h, p, planes)
                for pack in packs:
                    pack(s + 1, h, p, f)
            if sends:
                send_all(s + 1, sends, v)

    def wait_all(kind, s):
        for u in range(len(units[s])):
            arrived(kind, s, u)

    def pack_y_low(s, h, p, f):
        pack_y(s, h, p, f, range(half - 1), range(half))

    def pack_y_high(s, h, p, f):
        pack_y(s, h, p, f, range(half - 1, cx), range(half, cx))

    def pack_y_all(s, h, p, f):
        pack_y(s, h, p, f, range(cx), range(cx))

    planes = range(cx)
    local(0, planes)
    fwd_arrived()
    wait_all(HA, 0)
    mixed(0, planes)
    stage(
        0,
        (XUP, YUP, YDN, CUP),
        range(half),
        (pack_down, pack_y_low),
        (CDN, XDN, YUP, YDN),
    )
    stage(
        0,
        (XDN, CDN),
        range(half, cx),
        (pack_up, pack_y_high),
        (CUP, XUP, YUP2, YDN2, HA),
    )
    wait_all(HA, 1)
    local(1, [0])
    mixed(1, [0])
    local(1, [cx - 1])
    mixed(1, [cx - 1])
    stage(1, (XUP, YUP, YDN, CUP), [0], (pack_down,), (CDN, XDN))
    local(1, range(1, cx - 1))
    mixed(1, range(1, cx - 1))
    stage(1, (XDN, YUP2, YDN2, CDN), [cx - 1], (pack_up,), (CUP, XUP))
    stage(1, (), range(1, cx - 1), (pack_y_all,), (YUP, YDN, HA))
    wait_all(HA, 2)
    local(2, planes)
    mixed(2, planes)
    stage(2, (XUP, YUP, YDN, CUP), range(cx - 1), (), ())
    stage(2, (XDN, CDN), [cx - 1], (), ())

    for x in range(cx):
        part[x] = masks[x] * grads[x]
    grad_copy = pltpu.make_async_remote_copy(
        src_ref=part,
        dst_ref=other,
        send_sem=grad_sem.at[0],
        recv_sem=grad_sem.at[1],
        device_id=mate,
        device_id_type=MESH,
    )
    grad_copy.start()
    fwd_copy.wait_send()
    all_sent()
    grad_copy.wait()
    gout[...] = part[...] + other[...]


def store_kernel(adjoint, gradient, out, gout, sem):
    copies = [
        pltpu.make_async_copy(adjoint, out, sem.at[0]),
        pltpu.make_async_copy(gradient, gout, sem.at[1]),
    ]
    for copy in copies:
        copy.start()
    for copy in copies:
        copy.wait()


def shards(
    size_x,
    size_y,
    forward_field,
    adjoint_source,
    permittivity,
    frequency,
    design_tiles,
    mix_pairs,
    pml_width,
):
    own = forward_field.shape[0]
    cx, cy, cz = permittivity.shape
    f32 = jnp.float32
    field = forward_field.shape
    everyone = (2 * own,) + field[1:]
    planes = (2 * own, cx, cy, cz)
    face_x = (ITERS, own, 2, 2, cy, cz)
    face_y = (ITERS, own, 2, cx, 2, cz)
    edge = (ITERS, own, 2, 1, cz)
    hbm = pl.BlockSpec(memory_space=pl.ANY)
    vmem = pl.BlockSpec(memory_space=pltpu.VMEM)
    mix = jnp.transpose(mix_pairs, (1, 2, 0))
    shapes = (
        [everyone] * 4
        + [field, (cx, cy, cz)]
        + [planes] * 4
        + [field, (cx, cy, cz), (cx, cy, cz)]
        + [face_x] * 3
        + [face_y] * 4
        + [edge] * 4
    )
    adjoint, gradient = pl.pallas_call(
        functools.partial(kernel, size_x, size_y),
        out_shape=(
            pltpu.VMEM(field, f32),
            pltpu.VMEM((cx, cy, cz), f32),
        ),
        in_specs=[hbm] * 7,
        out_specs=(vmem, vmem),
        scratch_shapes=[
            pltpu.SMEM(frequency.shape, f32),
            pltpu.SMEM(design_tiles.shape, jnp.int32),
            pltpu.SMEM(mix.shape, jnp.int32),
            pltpu.SMEM(pml_width.shape, jnp.int32),
        ]
        + [pltpu.VMEM(shape, f32) for shape in shapes]
        + [
            pltpu.SemaphoreType.DMA((2 + own,)),
            pltpu.SemaphoreType.DMA((HA + ITERS,)),
            pltpu.SemaphoreType.DMA((len(recv_slots(own)),)),
            pltpu.SemaphoreType.DMA((2,)),
            pltpu.SemaphoreType.DMA((2,)),
            pltpu.SemaphoreType.DMA((4,)),
        ],
        compiler_params=pltpu.CompilerParams(collective_id=0, has_side_effects=True),
    )(
        forward_field,
        adjoint_source,
        permittivity,
        frequency,
        design_tiles,
        mix,
        pml_width,
    )
    return pl.pallas_call(
        store_kernel,
        out_shape=(
            jax.ShapeDtypeStruct(field, f32),
            jax.ShapeDtypeStruct((cx, cy, cz), f32),
        ),
        in_specs=[hbm, hbm],
        out_specs=(hbm, hbm),
        scratch_shapes=[pltpu.SemaphoreType.DMA((2,))],
        compiler_params=pltpu.CompilerParams(vmem_limit_bytes=1 << 20),
    )(adjoint, gradient)


def solution(mesh):
    return jax.shard_map(
        functools.partial(shards, mesh.shape["gx"], mesh.shape["gy"]),
        mesh=mesh,
        in_specs=(
            P("ha", None, None, ("cand", "gx"), "gy", None),
            P("ha", None, None, ("cand", "gx"), "gy", None),
            P(("cand", "gx"), "gy", None),
            P(),
            P(("cand", "gx"), "gy"),
            P(),
            P(),
        ),
        out_specs=(P("ha", None, None, ("cand", "gx"), "gy", None), P(("cand", "gx"), "gy", None)),
        check_vma=False,
    )
```

```python
import functools

import jax
import jax.numpy as jnp
from jax import lax
from jax.experimental import pallas as pl
from jax.experimental.pallas import tpu as pltpu
from jax.sharding import PartitionSpec as P

ITERS = 3
TILE = 4
PAIRS = 3

kerr_coef = 4.0
sigma_peak = 8.0

MESH = pl.DeviceIdType.MESH
XUP, XDN, YUP, YDN, CUP, CDN, HA = range(7)
YUP2, YDN2 = 12, 13
GRAIN = {XUP: 2, XDN: 2, YUP: 2, YDN: 2, CUP: 2, CDN: 2, HA: 2, YUP2: 2, YDN2: 2}


def cut(own, kind):
    cells = [(h, p) for h in range(own) for p in range(2)]
    size = len(cells) if GRAIN[kind] == 1 else 2
    return [cells[i : i + size] for i in range(0, len(cells), size)]


def recv_slots(own):
    messages = [(kind, s) for s in range(ITERS) for kind in range(7)] + [(YUP2, 1), (YDN2, 1)]
    slots = [(kind, s, u) for kind, s in messages for u in range(len(cut(own, kind)))]
    return {message: at for at, message in enumerate(slots)}


def kernel(
    size_x,
    size_y,
    fwd,
    src_hbm,
    perm_hbm,
    freq_hbm,
    tiles_hbm,
    mix_hbm,
    pml_hbm,
    out,
    gout,
    freq,
    tiles,
    mix,
    pml,
    fall,
    v0,
    v1,
    v2,
    src,
    perm,
    inv,
    gain,
    loss,
    kmask,
    held,
    part,
    other,
    xup_s,
    xup_r,
    xdn_r,
    yup_s,
    yup_r,
    ydn_s,
    ydn_r,
    cup_s,
    cup_r,
    cdn_s,
    cdn_r,
    load_sem,
    send_sem,
    recv_sem,
    fwd_sem,
    scalar_sem,
):
    own, _, _, cx, cy, cz = src.shape
    vs = (v0, v1, v2)
    gx = lax.axis_index("gx")
    gy = lax.axis_index("gy")
    ha = lax.axis_index("ha")
    has_xm, has_xp = gx > 0, gx < size_x - 1
    has_ym, has_yp = gy > 0, gy < size_y - 1
    xm, xp = jnp.maximum(gx - 1, 0), jnp.minimum(gx + 1, size_x - 1)
    ym, yp = jnp.maximum(gy - 1, 0), jnp.minimum(gy + 1, size_y - 1)
    mate = {"ha": 1 - ha}
    mine, theirs = ha * own, (1 - ha) * own
    made = (mine, theirs, theirs)
    work = (theirs, theirs, mine)

    load_scalars = [
        pltpu.make_async_copy(source, target, scalar_sem.at[i])
        for i, (source, target) in enumerate(
            ((freq_hbm, freq), (pml_hbm, pml), (tiles_hbm, tiles), (mix_hbm, mix))
        )
    ]
    load_perm = pltpu.make_async_copy(perm_hbm, perm, load_sem.at[0])
    load_src = [
        pltpu.make_async_copy(src_hbm.at[h], src.at[h], load_sem.at[1 + h]) for h in range(own)
    ]
    load_fwd = pltpu.make_async_copy(fwd, fall.at[pl.ds(mine, own)], load_sem.at[1 + own])
    load_scalars[0].start()
    load_perm.start()
    for copy in load_src:
        copy.start()

    barrier = pltpu.get_barrier_semaphore()
    peers = (
        (has_xp, {"gx": xp}),
        (has_xm, {"gx": xm}),
        (has_yp, {"gy": yp}),
        (has_ym, {"gy": ym}),
        (has_xp & has_ym, {"gx": xp, "gy": ym}),
        (has_xm & has_yp, {"gx": xm, "gy": yp}),
    )
    pl.semaphore_signal(barrier, inc=1, device_id=mate, device_id_type=MESH)
    count = jnp.int32(1)
    for there, peer in peers:
        count = count + there.astype(jnp.int32)

        @pl.when(there)
        def _():
            pl.semaphore_signal(barrier, inc=1, device_id=peer | mate, device_id_type=MESH)

    for copy in load_scalars[1:]:
        copy.start()
    load_fwd.start()

    units = cut(own, XUP)
    slots = recv_slots(own)
    every, low, high = pl.ds(0, cx), pl.ds(0, cx - 1), pl.ds(cx - 1, 1)
    low_up, high_up = pl.ds(0, cx - 2), pl.ds(cx - 2, 2)

    def which(kind, u, base=0):
        h, _ = cut(own, kind)[u][0]
        return (base + h if GRAIN[kind] == 2 else pl.ds(base, own)), slice(None)

    def spot(ref, s, kind, u, rows=None):
        return ref.at[(s,) + which(kind, u) + (() if rows is None else (rows,))]

    def block(v, kind, base, u, tail):
        return v.at[which(kind, u, base) + tail]

    def link(kind, s, u):
        v = vs[s]
        to = mate if work[s] is not made[s] else {}
        parted = s == 1
        first_up, first = (low_up, low) if parted else (every, every)
        if kind == HA:
            source = target = block(v, HA, made[s], u, (slice(None),))
            peer, sends, gets = mate, None, None
        else:
            face, halo, rows, peer, sends, gets = {
                XUP: (xup_s, xup_r, None, {"gx": xp}, has_xp, has_xm),
                XDN: (None, xdn_r, None, {"gx": xm}, has_xm, has_xp),
                YUP: (yup_s, yup_r, first_up, {"gy": yp}, has_yp, has_ym),
                YDN: (ydn_s, ydn_r, first, {"gy": ym}, has_ym, has_yp),
                YUP2: (yup_s, yup_r, high_up, {"gy": yp}, has_yp, has_ym),
                YDN2: (ydn_s, ydn_r, high, {"gy": ym}, has_ym, has_yp),
                CUP: (cup_s, cup_r, None, {"gx": xp, "gy": ym}, has_xp & has_ym, has_xm & has_yp),
                CDN: (cdn_s, cdn_r, None, {"gx": xm, "gy": yp}, has_xm & has_yp, has_xp & has_ym),
            }[kind]
            peer = peer | to
            target = spot(halo, s, kind, u, rows)
            if kind == XDN:
                source = block(v, XDN, made[s], u, (pl.ds(1, 2), 0))
            else:
                source = spot(face, s, kind, u, rows)
        copy = pltpu.make_async_remote_copy(
            src_ref=source,
            dst_ref=target,
            send_sem=send_sem.at[kind % 10],
            recv_sem=recv_sem.at[slots[kind, s, u]],
            device_id=peer,
            device_id_type=MESH,
        )
        return copy, sends, gets

    def send(kind, s, u):
        copy, sends, _ = link(kind, s, u)
        if sends is None:
            copy.start()
        else:
            pl.when(sends)(copy.start)

    def all_sent():
        for kind, halo in enumerate((xup_r, xdn_r, yup_r, ydn_r, cup_r, cdn_r)):
            copy, sends, _ = link(kind, 0, 0)
            total = pltpu.make_async_remote_copy(
                src_ref=halo,
                dst_ref=halo,
                send_sem=send_sem.at[kind],
                recv_sem=recv_sem.at[0],
                device_id=mate,
                device_id_type=MESH,
            )
            pl.when(sends)(total.wait_send)

    def mate_has(s):
        total = vs[s].at[pl.ds(made[s], own)]
        pltpu.make_async_remote_copy(
            src_ref=total,
            dst_ref=total,
            send_sem=send_sem.at[HA],
            recv_sem=recv_sem.at[0],
            device_id=mate,
            device_id_type=MESH,
        ).wait_send()

    def arrived(kind, s, u):
        if kind == HA:
            place = block(vs[s], HA, own - made[s], u, (slice(None),))
            pltpu.make_async_remote_copy(
                src_ref=place,
                dst_ref=place,
                send_sem=send_sem.at[HA],
                recv_sem=recv_sem.at[slots[kind, s, u]],
                device_id=mate,
                device_id_type=MESH,
            ).wait_recv()
        else:
            copy, _, gets = link(kind, s, u)
            pl.when(gets)(copy.wait_recv)

    iy = lax.broadcasted_iota(jnp.int32, (cy, cz), 0)
    iz = lax.broadcasted_iota(jnp.int32, (cy, cz), 1)
    keep_x = has_xm.astype(jnp.float32)
    keep_y = has_ym.astype(jnp.float32)

    def z_ahead(f):
        return jnp.where(iz == cz - 1, 0.0, pltpu.roll(f, cz - 1, 1))

    def z_behind(f):
        return jnp.where(iz == 0, 0.0, pltpu.roll(f, 1, 1))

    def y_ahead(f, row):
        return jnp.where(iy == cy - 1, row, pltpu.roll(f, cy - 1, 0))

    def y_behind(f, row):
        return jnp.where(iy == 0, row, pltpu.roll(f, 1, 0))

    def profile(width, extent, place):
        reach = jnp.maximum(jnp.maximum(width - place, place - (extent - 1 - width)), 0)
        ratio = reach.astype(jnp.float32) / jnp.full((cy, cz), width).astype(jnp.float32)
        return ratio * ratio

    def pack_up(s, h, p, f):
        fx, fy, fz = (f(c, cx - 1) for c in range(3))
        cup_s[s, h, p] = fx[0:1]
        xup_s[s, h, p, 0] = fy + y_ahead(fx, 0.0) - fx
        xup_s[s, h, p, 1] = fz + z_ahead(fx) - fx

    def pack_down(s, h, p, f):
        cdn_s[s, h, p] = f(1, 0)[cy - 1 : cy]

    def pack_y(s, h, p, f, up, down):
        for x in up:
            fx, fy, fz = (f(c, x)[cy - 1 : cy] for c in range(3))
            ahead = f(1, x + 1)[cy - 1 : cy] if x < cx - 1 else 0.0
            row_z = jnp.where(iz[0:1] == cz - 1, 0.0, pltpu.roll(fy, cz - 1, 1))
            yup_s[s, h, p, x, 0:1, :] = fx + ahead - fy
            yup_s[s, h, p, x, 1:2, :] = fz + row_z - fy
        for x in down:
            ydn_s[s, h, p, x, 0:1, :] = f(0, x)[0:1]
            ydn_s[s, h, p, x, 1:2, :] = f(2, x)[0:1]

    def send_all(s, kinds, unit):
        for kind in kinds:
            for u, cells in enumerate(cut(own, kind)):
                if cells[-1] in unit:
                    send(kind, s, u)

    load_scalars[0].wait()
    squared = [freq[i] * freq[i] for i in range(2 * own)]
    squared_mine = [freq[mine + h] * freq[mine + h] for h in range(own)]
    load_perm.wait()
    scales = {}
    for h in range(own):
        for x in range(cx):
            scales[h, x] = 1.0 / (10.0 + squared_mine[h] * perm[x])
    for h in range(own):
        load_src[h].wait()
        for p in range(2):
            f = {}
            for x in range(cx):
                for c in range(3):
                    f[c, x] = src[h, p, c, x] * scales[h, x]
                    v0[mine + h, p, c, x] = f[c, x]
            take = lambda c, x: f[c, x]
            pack_up(0, h, p, take)
            pack_down(0, h, p, take)
            pack_y(0, h, p, take, range(cx), range(cx))

    pl.semaphore_wait(barrier, count)
    for unit in units:
        send_all(0, (CUP, CDN, XUP, XDN, YUP, YDN), unit)
    for unit in units:
        send_all(0, (HA,), unit)
    fwd_copy = pltpu.make_async_remote_copy(
        src_ref=fwd,
        dst_ref=fall.at[pl.ds(mine, own)],
        send_sem=fwd_sem.at[0],
        recv_sem=fwd_sem.at[1],
        device_id=mate,
        device_id_type=MESH,
    )
    fwd_copy.start()

    for there, halo in (
        (has_xm, xup_r),
        (has_xp, xdn_r),
        (has_ym, yup_r),
        (has_yp, ydn_r),
        (has_xm & has_yp, cup_r),
        (has_xp & has_ym, cdn_r),
    ):

        @pl.when(jnp.logical_not(there))
        def _():
            halo[...] = jnp.zeros_like(halo)

    for copy in load_scalars[1:]:
        copy.wait()
    sigma_yz = profile(pml[1], cy * size_y, gy * cy + iy) + profile(pml[2], cz, iz)
    masks = []
    for x in range(cx):
        place = jnp.full((cy, cz), gx * cx + x)
        sigma = sigma_peak * (profile(pml[0], cx * size_x, place) + sigma_yz)
        mask = jnp.zeros((cy, cz), jnp.float32)
        for t in range(cy // TILE):
            inside = (iy >= t * TILE) & (iy < (t + 1) * TILE)
            mask = jnp.where(inside, tiles[x // TILE, t].astype(jnp.float32), mask)
        for i in range(2 * own):
            weighed = squared[i] * perm[x]
            inv[i, x] = 1.0 / (10.0 + weighed)
            gain[i, x] = 10.0 + 2.0 * weighed
            loss[i, x] = squared[i] * sigma
            kmask[i, x] = (kerr_coef * squared[i]) * mask
        masks.append(mask)

    def fwd_arrived():
        load_fwd.wait()
        pltpu.make_async_remote_copy(
            src_ref=fwd,
            dst_ref=fall.at[pl.ds(theirs, own)],
            send_sem=fwd_sem.at[0],
            recv_sem=fwd_sem.at[1],
            device_id=mate,
            device_id_type=MESH,
        ).wait_recv()

    grads = {}

    def local(s, planes):
        v = vs[s]
        base = work[s]
        for h in range(own):
            gh = base + h
            for p in range(2):
                field = lambda c, x: v[gh, p, c, x]
                mz_behind = my_behind = None
                for x in planes:
                    fx, fy, fz = field(0, x), field(1, x), field(2, x)
                    fy_ahead = field(1, x + 1) if x < cx - 1 else 0.0
                    fz_ahead = field(2, x + 1) if x < cx - 1 else 0.0
                    mx = (y_ahead(fz, 0.0) - fz) - (z_ahead(fy) - fy)
                    my = (z_ahead(fx) - fx) - (fz_ahead - fz)
                    mz = (fy_ahead - fy) - (y_ahead(fx, 0.0) - fx)
                    if x == 0:
                        mz_behind, my_behind = keep_x * fy, -keep_x * fz
                    elif mz_behind is None:
                        bx, by, bz = (field(c, x - 1) for c in range(3))
                        my_behind = (z_ahead(bx) - bx) - (fz - bz)
                        mz_behind = (fy - by) - (y_ahead(bx, 0.0) - bx)
                    mz_low = y_behind(mz, -keep_y * fx)
                    mx_low = y_behind(mx, keep_y * fz)
                    curls = (
                        (mz - mz_low) - (my - z_behind(my)),
                        (mx - z_behind(mx)) - (mz - mz_behind),
                        (my - my_behind) - (mx - mx_low),
                    )
                    my_behind, mz_behind = my, mz
                    k1, k2 = gain[gh, x], loss[gh, x]
                    scale = 0.5 * k1 + 5.0
                    for c, at_c in enumerate((fx, fy, fz)):
                        turned = k2 * v[gh, 1 - p, c, x]
                        turned = -turned if p == 0 else turned
                        given = src[h, p, c, x] if base is mine else v0[gh, p, c, x] * scale
                        held[h, p, c, x] = given + k1 * at_c + turned - curls[c]

    def mixed(s, planes):
        v = vs[s]
        base = work[s]
        for h in range(own):
            firsts = [mix[k, 0, base + h] for k in range(PAIRS)]
            seconds = [mix[k, 1, base + h] for k in range(PAIRS)]
            for x in planes:
                k3 = kmask[base + h, x]
                for c in range(3):
                    real = imag = None
                    for a, b in zip(firsts, seconds):
                        fr, fi = fall[a, 0, c, x], fall[a, 1, c, x]
                        vr, vi = v[b, 0, c, x], v[b, 1, c, x]
                        re, im = fr * vr - fi * vi, fr * vi + fi * vr
                        real = re if real is None else real + re
                        imag = im if imag is None else imag + im
                    held[h, 0, c, x] = held[h, 0, c, x] + k3 * real
                    held[h, 1, c, x] = held[h, 1, c, x] + k3 * imag

    def finish(s, h, p, planes):
        gh = work[s] + h
        f = {}
        for x in planes:
            scale = inv[gh, x]
            row = lambda ref, c, at: ref[s, h, p, at, c : c + 1, :]
            fx_next, fz_next = row(ydn_r, 0, x), row(ydn_r, 1, x)
            low_z, low_x = row(yup_r, 0, x), row(yup_r, 1, x)
            if x == cx - 1:
                low_z = low_z + cdn_r[s, h, p]
            fx_prev = row(ydn_r, 0, x - 1) if x > 0 else cup_r[s, h, p]
            fz_step = fz_next - jnp.where(iz[0:1] == 0, 0.0, pltpu.roll(fz_next, 1, 1))
            less_x = jnp.where(iy == 0, low_z, jnp.where(iy == cy - 1, fx_next, 0.0))
            less_y = jnp.where(iy == cy - 1, fx_prev - fx_next - fz_step, 0.0)
            less_z = jnp.where(iy == 0, low_x, jnp.where(iy == cy - 1, fz_next, 0.0))
            if x == 0:
                less_y = less_y + xup_r[s, h, p, 0]
                less_z = less_z + xup_r[s, h, p, 1]
            if x == cx - 1:
                fy_ahead, fz_ahead = xdn_r[s, h, p, 0], xdn_r[s, h, p, 1]
                steps = (fy_ahead - y_behind(fy_ahead, 0.0)) + (fz_ahead - z_behind(fz_ahead))
                less_x = less_x - steps
                less_y = less_y + fy_ahead
                less_z = less_z + fz_ahead
            total = None
            for c, less in enumerate((less_x, less_y, less_z)):
                new = scale * (held[h, p, c, x] + less)
                f[c, x] = new
                if s < ITERS - 1:
                    vs[s + 1][gh, p, c, x] = new
                else:
                    out[h, p, c, x] = new
                    term = new * fall[gh, p, c, x]
                    total = term if total is None else total + term
            if s == ITERS - 1:
                total = (squared_mine[h] if p == 0 else -squared_mine[h]) * total
                grads[x] = grads[x] + total if x in grads else total
        if s == ITERS - 1:
            return None
        v = vs[s + 1]
        return lambda c, x: f[c, x] if (c, x) in f else v[gh, p, c, x]

    def stage(s, waits, planes, steps):
        for unit in units:
            for kind in waits:
                for u, cells in enumerate(cut(own, kind)):
                    if cells[0] in unit:
                        arrived(kind, s, u)
            fields = [(h, p, finish(s, h, p, planes)) for h, p in unit]
            for pack, kinds in steps:
                for h, p, f in fields:
                    if pack is not None:
                        pack(s + 1, h, p, f)
                send_all(s + 1, kinds, unit)

    def wait_all(kind, s):
        for u in range(len(cut(own, kind))):
            arrived(kind, s, u)

    def pack_y_low(s, h, p, f):
        pack_y(s, h, p, f, range(cx - 2), range(cx - 1))

    def pack_y_high(s, h, p, f):
        pack_y(s, h, p, f, range(cx - 2, cx), [cx - 1])

    planes, inner = range(cx), range(1, cx - 1)
    wait_all(HA, 0)
    local(0, planes)
    fwd_arrived()
    mixed(0, planes)
    stage(0, (XUP, CUP, YUP, YDN), [0], [(pack_down, (CDN, XDN))])
    stage(0, (), inner, [(pack_y_low, (YUP, YDN))])
    stage(0, (XDN, CDN), [cx - 1], [(pack_up, (CUP, XUP)), (pack_y_high, (YUP2, YDN2))])
    mate_has(0)
    for unit in units:
        send_all(1, (HA,), unit)
    local(1, [0])
    local(1, [cx - 1])
    wait_all(HA, 1)
    mixed(1, [0])
    mixed(1, [cx - 1])
    stage(1, (XUP, CUP, YUP, YDN), [0], [(pack_down, (CDN, XDN))])
    local(1, inner)
    mixed(1, inner)
    stage(1, (YUP2, YDN2), inner, [(pack_y_low, ())])
    stage(1, (XDN, CDN), [cx - 1], [(pack_up, (CUP, XUP)), (pack_y_high, (YUP, YDN))])
    mate_has(1)
    for unit in units:
        send_all(2, (HA,), unit)
    fwd_copy.wait_send()
    wait_all(HA, 2)
    local(2, planes)
    mixed(2, planes)
    stage(2, (XUP, CUP, YUP, YDN), range(cx - 1), [])
    stage(2, (XDN, CDN), [cx - 1], [])
    mate_has(2)

    for x in range(cx):
        part[x] = masks[x] * grads[x]
    grad_copy = pltpu.make_async_remote_copy(
        src_ref=part,
        dst_ref=other,
        send_sem=fwd_sem.at[0],
        recv_sem=fwd_sem.at[1],
        device_id=mate,
        device_id_type=MESH,
    )
    grad_copy.start()
    all_sent()
    grad_copy.wait()
    gout[...] = part[...] + other[...]


def store_kernel(adjoint, gradient, out, gout, sem):
    copies = [
        pltpu.make_async_copy(adjoint, out, sem.at[0]),
        pltpu.make_async_copy(gradient, gout, sem.at[1]),
    ]
    for copy in copies:
        copy.start()
    for copy in copies:
        copy.wait()


def shards(
    size_x,
    size_y,
    forward_field,
    adjoint_source,
    permittivity,
    frequency,
    design_tiles,
    mix_pairs,
    pml_width,
):
    own = forward_field.shape[0]
    cx, cy, cz = permittivity.shape
    f32 = jnp.float32
    field = forward_field.shape
    everyone = (2 * own,) + field[1:]
    planes = (2 * own, cx, cy, cz)
    face_x = (ITERS, own, 2, 2, cy, cz)
    face_y = (ITERS, own, 2, cx, 2, cz)
    edge = (ITERS, own, 2, 1, cz)
    hbm = pl.BlockSpec(memory_space=pl.ANY)
    vmem = pl.BlockSpec(memory_space=pltpu.VMEM)
    mix = jnp.transpose(mix_pairs, (1, 2, 0))
    shapes = (
        [everyone] * 4
        + [field, (cx, cy, cz)]
        + [planes] * 4
        + [field, (cx, cy, cz), (cx, cy, cz)]
        + [face_x] * 3
        + [face_y] * 4
        + [edge] * 4
    )
    adjoint, gradient = pl.pallas_call(
        functools.partial(kernel, size_x, size_y),
        out_shape=(
            pltpu.VMEM(field, f32),
            pltpu.VMEM((cx, cy, cz), f32),
        ),
        in_specs=[hbm] * 7,
        out_specs=(vmem, vmem),
        scratch_shapes=[
            pltpu.SMEM(frequency.shape, f32),
            pltpu.SMEM(design_tiles.shape, jnp.int32),
            pltpu.SMEM(mix.shape, jnp.int32),
            pltpu.SMEM(pml_width.shape, jnp.int32),
        ]
        + [pltpu.VMEM(shape, f32) for shape in shapes]
        + [
            pltpu.SemaphoreType.DMA((2 + own,)),
            pltpu.SemaphoreType.DMA((HA + 1,)),
            pltpu.SemaphoreType.DMA((len(recv_slots(own)),)),
            pltpu.SemaphoreType.DMA((2,)),
            pltpu.SemaphoreType.DMA((4,)),
        ],
        compiler_params=pltpu.CompilerParams(collective_id=0, has_side_effects=True),
    )(
        forward_field,
        adjoint_source,
        permittivity,
        frequency,
        design_tiles,
        mix,
        pml_width,
    )
    return pl.pallas_call(
        store_kernel,
        out_shape=(
            jax.ShapeDtypeStruct(field, f32),
            jax.ShapeDtypeStruct((cx, cy, cz), f32),
        ),
        in_specs=[hbm, hbm],
        out_specs=(hbm, hbm),
        scratch_shapes=[pltpu.SemaphoreType.DMA((2,))],
        compiler_params=pltpu.CompilerParams(vmem_limit_bytes=1 << 20),
    )(adjoint, gradient)


def solution(mesh):
    return jax.shard_map(
        functools.partial(shards, mesh.shape["gx"], mesh.shape["gy"]),
        mesh=mesh,
        in_specs=(
            P("ha", None, None, ("cand", "gx"), "gy", None),
            P("ha", None, None, ("cand", "gx"), "gy", None),
            P(("cand", "gx"), "gy", None),
            P(),
            P(("cand", "gx"), "gy"),
            P(),
            P(),
        ),
        out_specs=(P("ha", None, None, ("cand", "gx"), "gy", None), P(("cand", "gx"), "gy", None)),
        check_vma=False,
    )
```

```python
import functools

import jax
import jax.numpy as jnp
from jax import lax
from jax.experimental import pallas as pl
from jax.experimental.pallas import tpu as pltpu
from jax.sharding import PartitionSpec as P

ITERS = 3
TILE = 4
PAIRS = 3

kerr_coef = 4.0
sigma_peak = 8.0

MESH = pl.DeviceIdType.MESH
XUP, XDN, YUP, YDN, CUP, CDN, HA = range(7)
YUP2, YDN2 = 12, 13
GRAIN = {XUP: 2, XDN: 2, YUP: 2, YDN: 2, CUP: 2, CDN: 2, HA: 2, YUP2: 2, YDN2: 2}


def cut(own, kind):
    cells = [(h, p) for h in range(own) for p in range(2)]
    size = len(cells) if GRAIN[kind] == 1 else 2
    return [cells[i : i + size] for i in range(0, len(cells), size)]


def recv_slots(own):
    messages = [(kind, s) for s in range(ITERS) for kind in range(7) if (kind, s) != (HA, 2)] + [(YUP2, 1), (YDN2, 1)]
    slots = [(kind, s, u) for kind, s in messages for u in range(len(cut(own, kind)))]
    return {message: at for at, message in enumerate(slots)}


def kernel(
    size_x,
    size_y,
    fwd,
    src_hbm,
    perm_hbm,
    freq_hbm,
    tiles_hbm,
    mix_hbm,
    pml_hbm,
    out,
    gout,
    freq,
    tiles,
    mix,
    pml,
    fall,
    v0,
    v1,
    v2,
    src,
    perm,
    inv,
    gain,
    loss,
    kmask,
    held,
    part,
    other,
    xup_s,
    xup_r,
    xdn_r,
    yup_s,
    yup_r,
    ydn_s,
    ydn_r,
    cup_s,
    cup_r,
    cdn_s,
    cdn_r,
    load_sem,
    send_sem,
    recv_sem,
    fwd_sem,
    scalar_sem,
):
    own, _, _, cx, cy, cz = src.shape
    vs = (v0, v1, v2)
    gx = lax.axis_index("gx")
    gy = lax.axis_index("gy")
    ha = lax.axis_index("ha")
    has_xm, has_xp = gx > 0, gx < size_x - 1
    has_ym, has_yp = gy > 0, gy < size_y - 1
    xm, xp = jnp.maximum(gx - 1, 0), jnp.minimum(gx + 1, size_x - 1)
    ym, yp = jnp.maximum(gy - 1, 0), jnp.minimum(gy + 1, size_y - 1)
    mate = {"ha": 1 - ha}
    mine, theirs = ha * own, (1 - ha) * own
    made = (mine, theirs, theirs)
    work = (theirs, theirs, mine)

    load_scalars = [
        pltpu.make_async_copy(source, target, scalar_sem.at[i])
        for i, (source, target) in enumerate(
            ((freq_hbm, freq), (pml_hbm, pml), (tiles_hbm, tiles), (mix_hbm, mix))
        )
    ]
    load_perm = pltpu.make_async_copy(perm_hbm, perm, load_sem.at[0])
    load_src = [
        pltpu.make_async_copy(src_hbm.at[h], src.at[h], load_sem.at[1 + h]) for h in range(own)
    ]
    load_fwd = pltpu.make_async_copy(fwd, fall.at[pl.ds(mine, own)], load_sem.at[1 + own])

    barrier = pltpu.get_barrier_semaphore()
    peers = (
        (has_xp, {"gx": xp}),
        (has_xm, {"gx": xm}),
        (has_yp, {"gy": yp}),
        (has_ym, {"gy": ym}),
        (has_xp & has_ym, {"gx": xp, "gy": ym}),
        (has_xm & has_yp, {"gx": xm, "gy": yp}),
    )
    pl.semaphore_signal(barrier, inc=1, device_id=mate, device_id_type=MESH)
    count = jnp.int32(1)
    for there, peer in peers:
        count = count + there.astype(jnp.int32)

        @pl.when(there)
        def _():
            pl.semaphore_signal(barrier, inc=1, device_id=peer | mate, device_id_type=MESH)

    load_scalars[0].start()
    load_perm.start()
    for copy in load_src:
        copy.start()
    for copy in load_scalars[1:]:
        copy.start()
    load_fwd.start()

    units = cut(own, XUP)
    slots = recv_slots(own)
    every, low, high = pl.ds(0, cx), pl.ds(0, cx - 1), pl.ds(cx - 1, 1)
    low_up, high_up = pl.ds(0, cx - 2), pl.ds(cx - 2, 2)

    def which(kind, u, base=0):
        h, _ = cut(own, kind)[u][0]
        return (base + h if GRAIN[kind] == 2 else pl.ds(base, own)), slice(None)

    def spot(ref, s, kind, u, rows=None):
        return ref.at[(s,) + which(kind, u) + (() if rows is None else (rows,))]

    def block(v, kind, base, u, tail):
        return v.at[which(kind, u, base) + tail]

    def link(kind, s, u):
        v = vs[s]
        to = mate if work[s] is not made[s] else {}
        parted = s == 1
        first_up, first = (low_up, low) if parted else (every, every)
        if kind == HA:
            source = target = block(v, HA, made[s], u, (slice(None),))
            peer, sends, gets = mate, None, None
        else:
            face, halo, rows, peer, sends, gets = {
                XUP: (xup_s, xup_r, None, {"gx": xp}, has_xp, has_xm),
                XDN: (None, xdn_r, None, {"gx": xm}, has_xm, has_xp),
                YUP: (yup_s, yup_r, first_up, {"gy": yp}, has_yp, has_ym),
                YDN: (ydn_s, ydn_r, first, {"gy": ym}, has_ym, has_yp),
                YUP2: (yup_s, yup_r, high_up, {"gy": yp}, has_yp, has_ym),
                YDN2: (ydn_s, ydn_r, high, {"gy": ym}, has_ym, has_yp),
                CUP: (cup_s, cup_r, None, {"gx": xp, "gy": ym}, has_xp & has_ym, has_xm & has_yp),
                CDN: (cdn_s, cdn_r, None, {"gx": xm, "gy": yp}, has_xm & has_yp, has_xp & has_ym),
            }[kind]
            peer = peer | to
            target = spot(halo, s, kind, u, rows)
            if kind == XDN:
                source = block(v, XDN, made[s], u, (pl.ds(1, 2), 0))
            else:
                source = spot(face, s, kind, u, rows)
        copy = pltpu.make_async_remote_copy(
            src_ref=source,
            dst_ref=target,
            send_sem=send_sem.at[kind % 10],
            recv_sem=recv_sem.at[slots[kind, s % 2 if kind == HA else s, u]],
            device_id=peer,
            device_id_type=MESH,
        )
        return copy, sends, gets

    def send(kind, s, u):
        copy, sends, _ = link(kind, s, u)
        if sends is None:
            copy.start()
        else:
            pl.when(sends)(copy.start)

    def all_sent():
        for kind, halo in enumerate((xup_r, xdn_r, yup_r, ydn_r, cup_r, cdn_r)):
            copy, sends, _ = link(kind, 0, 0)
            total = pltpu.make_async_remote_copy(
                src_ref=halo,
                dst_ref=halo,
                send_sem=send_sem.at[kind],
                recv_sem=recv_sem.at[0],
                device_id=mate,
                device_id_type=MESH,
            )
            pl.when(sends)(total.wait_send)

    def mate_has(s):
        total = vs[s].at[pl.ds(made[s], own)]
        pltpu.make_async_remote_copy(
            src_ref=total,
            dst_ref=total,
            send_sem=send_sem.at[HA],
            recv_sem=recv_sem.at[0],
            device_id=mate,
            device_id_type=MESH,
        ).wait_send()

    def arrived(kind, s, u):
        if kind == HA:
            place = block(vs[s], HA, own - made[s], u, (slice(None),))
            pltpu.make_async_remote_copy(
                src_ref=place,
                dst_ref=place,
                send_sem=send_sem.at[HA],
                recv_sem=recv_sem.at[slots[kind, s % 2 if kind == HA else s, u]],
                device_id=mate,
                device_id_type=MESH,
            ).wait_recv()
        else:
            copy, _, gets = link(kind, s, u)
            pl.when(gets)(copy.wait_recv)

    iy = lax.broadcasted_iota(jnp.int32, (cy, cz), 0)
    iz = lax.broadcasted_iota(jnp.int32, (cy, cz), 1)
    keep_x = has_xm.astype(jnp.float32)
    keep_y = has_ym.astype(jnp.float32)

    def z_ahead(f):
        return jnp.where(iz == cz - 1, 0.0, pltpu.roll(f, cz - 1, 1))

    def z_behind(f):
        return jnp.where(iz == 0, 0.0, pltpu.roll(f, 1, 1))

    def y_ahead(f, row):
        return jnp.where(iy == cy - 1, row, pltpu.roll(f, cy - 1, 0))

    def y_behind(f, row):
        return jnp.where(iy == 0, row, pltpu.roll(f, 1, 0))

    def profile(width, extent, place):
        reach = jnp.maximum(jnp.maximum(width - place, place - (extent - 1 - width)), 0)
        ratio = reach.astype(jnp.float32) / jnp.full((cy, cz), width).astype(jnp.float32)
        return ratio * ratio

    def pack_up(s, h, p, f):
        fx, fy, fz = (f(c, cx - 1) for c in range(3))
        cup_s[s, h, p] = fx[0:1]
        xup_s[s, h, p, 0] = fy + y_ahead(fx, 0.0) - fx
        xup_s[s, h, p, 1] = fz + z_ahead(fx) - fx

    def pack_down(s, h, p, f):
        cdn_s[s, h, p] = f(1, 0)[cy - 1 : cy]

    def pack_y(s, h, p, f, up, down):
        for x in up:
            fx, fy, fz = (f(c, x)[cy - 1 : cy] for c in range(3))
            ahead = f(1, x + 1)[cy - 1 : cy] if x < cx - 1 else 0.0
            row_z = jnp.where(iz[0:1] == cz - 1, 0.0, pltpu.roll(fy, cz - 1, 1))
            yup_s[s, h, p, x, 0:1, :] = fx + ahead - fy
            yup_s[s, h, p, x, 1:2, :] = fz + row_z - fy
        for x in down:
            ydn_s[s, h, p, x, 0:1, :] = f(0, x)[0:1]
            ydn_s[s, h, p, x, 1:2, :] = f(2, x)[0:1]

    def send_all(s, kinds, unit):
        for kind in kinds:
            for u, cells in enumerate(cut(own, kind)):
                if cells[-1] in unit:
                    send(kind, s, u)

    load_scalars[0].wait()
    squared = [freq[i] * freq[i] for i in range(2 * own)]
    squared_mine = [freq[mine + h] * freq[mine + h] for h in range(own)]
    load_perm.wait()
    scales = {}
    for h in range(own):
        for x in range(cx):
            scales[h, x] = 1.0 / (10.0 + squared_mine[h] * perm[x])
    for h in range(own):
        load_src[h].wait()
        for p in range(2):
            f = {}
            for x in range(cx):
                for c in range(3):
                    f[c, x] = src[h, p, c, x] * scales[h, x]
                    v0[mine + h, p, c, x] = f[c, x]
            take = lambda c, x: f[c, x]
            pack_up(0, h, p, take)
            pack_down(0, h, p, take)
            pack_y(0, h, p, take, range(cx), range(cx))

    pl.semaphore_wait(barrier, count)
    for unit in units:
        send_all(0, (CUP, CDN, XUP, XDN, YUP, YDN), unit)
    for unit in units:
        send_all(0, (HA,), unit)
    fwd_copy = pltpu.make_async_remote_copy(
        src_ref=fwd,
        dst_ref=fall.at[pl.ds(mine, own)],
        send_sem=fwd_sem.at[0],
        recv_sem=fwd_sem.at[1],
        device_id=mate,
        device_id_type=MESH,
    )
    fwd_copy.start()

    for there, halo in (
        (has_xm, xup_r),
        (has_xp, xdn_r),
        (has_ym, yup_r),
        (has_yp, ydn_r),
        (has_xm & has_yp, cup_r),
        (has_xp & has_ym, cdn_r),
    ):

        @pl.when(jnp.logical_not(there))
        def _():
            halo[...] = jnp.zeros_like(halo)

    for copy in load_scalars[1:]:
        copy.wait()
    sigma_yz = profile(pml[1], cy * size_y, gy * cy + iy) + profile(pml[2], cz, iz)
    masks = []
    for x in range(cx):
        place = jnp.full((cy, cz), gx * cx + x)
        sigma = sigma_peak * (profile(pml[0], cx * size_x, place) + sigma_yz)
        mask = jnp.zeros((cy, cz), jnp.float32)
        for t in range(cy // TILE):
            inside = (iy >= t * TILE) & (iy < (t + 1) * TILE)
            mask = jnp.where(inside, tiles[x // TILE, t].astype(jnp.float32), mask)
        for i in range(2 * own):
            weighed = squared[i] * perm[x]
            inv[i, x] = 1.0 / (10.0 + weighed)
            gain[i, x] = 10.0 + 2.0 * weighed
            loss[i, x] = squared[i] * sigma
            kmask[i, x] = (kerr_coef * squared[i]) * mask
        masks.append(mask)

    def fwd_arrived():
        load_fwd.wait()
        pltpu.make_async_remote_copy(
            src_ref=fwd,
            dst_ref=fall.at[pl.ds(theirs, own)],
            send_sem=fwd_sem.at[0],
            recv_sem=fwd_sem.at[1],
            device_id=mate,
            device_id_type=MESH,
        ).wait_recv()

    grads = {}

    def local(s, planes):
        v = vs[s]
        base = work[s]
        for h in range(own):
            gh = base + h
            for p in range(2):
                field = lambda c, x: v[gh, p, c, x]
                mz_behind = my_behind = None
                for x in planes:
                    fx, fy, fz = field(0, x), field(1, x), field(2, x)
                    fy_ahead = field(1, x + 1) if x < cx - 1 else 0.0
                    fz_ahead = field(2, x + 1) if x < cx - 1 else 0.0
                    mx = (y_ahead(fz, 0.0) - fz) - (z_ahead(fy) - fy)
                    my = (z_ahead(fx) - fx) - (fz_ahead - fz)
                    mz = (fy_ahead - fy) - (y_ahead(fx, 0.0) - fx)
                    if x == 0:
                        mz_behind, my_behind = keep_x * fy, -keep_x * fz
                    elif mz_behind is None:
                        bx, by, bz = (field(c, x - 1) for c in range(3))
                        my_behind = (z_ahead(bx) - bx) - (fz - bz)
                        mz_behind = (fy - by) - (y_ahead(bx, 0.0) - bx)
                    mz_low = y_behind(mz, -keep_y * fx)
                    mx_low = y_behind(mx, keep_y * fz)
                    curls = (
                        (mz - mz_low) - (my - z_behind(my)),
                        (mx - z_behind(mx)) - (mz - mz_behind),
                        (my - my_behind) - (mx - mx_low),
                    )
                    my_behind, mz_behind = my, mz
                    k1, k2 = gain[gh, x], loss[gh, x]
                    scale = 0.5 * k1 + 5.0
                    for c, at_c in enumerate((fx, fy, fz)):
                        turned = k2 * v[gh, 1 - p, c, x]
                        turned = -turned if p == 0 else turned
                        given = src[h, p, c, x] if base is mine else v0[gh, p, c, x] * scale
                        held[h, p, c, x] = given + k1 * at_c + turned - curls[c]

    def mixed(s, planes):
        v = vs[s]
        base = work[s]
        for h in range(own):
            firsts = [mix[k, 0, base + h] for k in range(PAIRS)]
            seconds = [mix[k, 1, base + h] for k in range(PAIRS)]
            for x in planes:
                k3 = kmask[base + h, x]
                for c in range(3):
                    real = imag = None
                    for a, b in zip(firsts, seconds):
                        fr, fi = fall[a, 0, c, x], fall[a, 1, c, x]
                        vr, vi = v[b, 0, c, x], v[b, 1, c, x]
                        re, im = fr * vr - fi * vi, fr * vi + fi * vr
                        real = re if real is None else real + re
                        imag = im if imag is None else imag + im
                    held[h, 0, c, x] = held[h, 0, c, x] + k3 * real
                    held[h, 1, c, x] = held[h, 1, c, x] + k3 * imag

    def finish(s, h, p, planes):
        gh = work[s] + h
        f = {}
        for x in planes:
            scale = inv[gh, x]
            row = lambda ref, c, at: ref[s, h, p, at, c : c + 1, :]
            fx_next, fz_next = row(ydn_r, 0, x), row(ydn_r, 1, x)
            low_z, low_x = row(yup_r, 0, x), row(yup_r, 1, x)
            if x == cx - 1:
                low_z = low_z + cdn_r[s, h, p]
            fx_prev = row(ydn_r, 0, x - 1) if x > 0 else cup_r[s, h, p]
            fz_step = fz_next - jnp.where(iz[0:1] == 0, 0.0, pltpu.roll(fz_next, 1, 1))
            less_x = jnp.where(iy == 0, low_z, jnp.where(iy == cy - 1, fx_next, 0.0))
            less_y = jnp.where(iy == cy - 1, fx_prev - fx_next - fz_step, 0.0)
            less_z = jnp.where(iy == 0, low_x, jnp.where(iy == cy - 1, fz_next, 0.0))
            if x == 0:
                less_y = less_y + xup_r[s, h, p, 0]
                less_z = less_z + xup_r[s, h, p, 1]
            if x == cx - 1:
                fy_ahead, fz_ahead = xdn_r[s, h, p, 0], xdn_r[s, h, p, 1]
                steps = (fy_ahead - y_behind(fy_ahead, 0.0)) + (fz_ahead - z_behind(fz_ahead))
                less_x = less_x - steps
                less_y = less_y + fy_ahead
                less_z = less_z + fz_ahead
            total = None
            for c, less in enumerate((less_x, less_y, less_z)):
                new = scale * (held[h, p, c, x] + less)
                f[c, x] = new
                if s < ITERS - 1:
                    vs[s + 1][gh, p, c, x] = new
                else:
                    out[h, p, c, x] = new
                    term = new * fall[gh, p, c, x]
                    total = term if total is None else total + term
            if s == ITERS - 1:
                total = (squared_mine[h] if p == 0 else -squared_mine[h]) * total
                grads[x] = grads[x] + total if x in grads else total
        if s == ITERS - 1:
            return None
        v = vs[s + 1]
        return lambda c, x: f[c, x] if (c, x) in f else v[gh, p, c, x]

    def stage(s, waits, planes, steps):
        for unit in units:
            for kind in waits:
                for u, cells in enumerate(cut(own, kind)):
                    if cells[0] in unit:
                        arrived(kind, s, u)
            fields = [(h, p, finish(s, h, p, planes)) for h, p in unit]
            for pack, kinds in steps:
                for h, p, f in fields:
                    if pack is not None:
                        pack(s + 1, h, p, f)
                send_all(s + 1, kinds, unit)

    def wait_all(kind, s):
        for u in range(len(cut(own, kind))):
            arrived(kind, s, u)

    def pack_y_low(s, h, p, f):
        pack_y(s, h, p, f, range(cx - 2), range(cx - 1))

    def pack_y_high(s, h, p, f):
        pack_y(s, h, p, f, range(cx - 2, cx), [cx - 1])

    shared = []

    def share(at, first, size):
        for x in range(first, first + size):
            part[x] = masks[x] * grads[x]
        copy = pltpu.make_async_remote_copy(
            src_ref=part.at[pl.ds(first, size)],
            dst_ref=other.at[pl.ds(first, size)],
            send_sem=fwd_sem.at[2 * at],
            recv_sem=fwd_sem.at[2 * at + 1],
            device_id=mate,
            device_id_type=MESH,
        )
        copy.start()
        shared.append(copy)

    planes, inner = range(cx), range(1, cx - 1)
    wait_all(HA, 0)
    local(0, planes)
    fwd_arrived()
    mixed(0, planes)
    stage(0, (XUP, CUP, YUP, YDN), [0], [(pack_down, (CDN, XDN))])
    stage(0, (), inner, [(pack_y_low, (YUP, YDN))])
    stage(0, (XDN, CDN), [cx - 1], [(pack_up, (CUP, XUP)), (pack_y_high, (YUP2, YDN2))])
    mate_has(0)
    for unit in units:
        send_all(1, (HA,), unit)
    local(1, [0])
    local(1, [cx - 1])
    wait_all(HA, 1)
    mixed(1, [0])
    mixed(1, [cx - 1])
    stage(1, (XUP, CUP, YUP, YDN), [0], [(pack_down, (CDN, XDN))])
    local(1, inner)
    mixed(1, inner)
    stage(1, (YUP2, YDN2), inner, [(pack_y_low, ())])
    stage(1, (XDN, CDN), [cx - 1], [(pack_up, (CUP, XUP)), (pack_y_high, (YUP, YDN))])
    mate_has(1)
    for unit in units:
        send_all(2, (HA,), unit)
    fwd_copy.wait_send()
    wait_all(HA, 2)
    local(2, planes)
    mixed(2, planes)
    stage(2, (XUP, CUP, YUP, YDN), range(cx - 1), [])
    share(0, 0, cx - 1)
    stage(2, (XDN, CDN), [cx - 1], [])
    mate_has(2)

    share(1, cx - 1, 1)
    all_sent()
    for copy in shared:
        copy.wait()
    gout[...] = part[...] + other[...]


def store_kernel(adjoint, gradient, out, gout, sem):
    copies = [
        pltpu.make_async_copy(adjoint, out, sem.at[0]),
        pltpu.make_async_copy(gradient, gout, sem.at[1]),
    ]
    for copy in copies:
        copy.start()
    for copy in copies:
        copy.wait()


def shards(
    size_x,
    size_y,
    forward_field,
    adjoint_source,
    permittivity,
    frequency,
    design_tiles,
    mix_pairs,
    pml_width,
):
    own = forward_field.shape[0]
    cx, cy, cz = permittivity.shape
    f32 = jnp.float32
    field = forward_field.shape
    everyone = (2 * own,) + field[1:]
    planes = (2 * own, cx, cy, cz)
    face_x = (ITERS, own, 2, 2, cy, cz)
    face_y = (ITERS, own, 2, cx, 2, cz)
    edge = (ITERS, own, 2, 1, cz)
    hbm = pl.BlockSpec(memory_space=pl.ANY)
    vmem = pl.BlockSpec(memory_space=pltpu.VMEM)
    mix = jnp.transpose(mix_pairs, (1, 2, 0))
    shapes = (
        [everyone] * 4
        + [field, (cx, cy, cz)]
        + [planes] * 4
        + [field, (cx, cy, cz), (cx, cy, cz)]
        + [face_x] * 3
        + [face_y] * 4
        + [edge] * 4
    )
    adjoint, gradient = pl.pallas_call(
        functools.partial(kernel, size_x, size_y),
        out_shape=(
            pltpu.VMEM(field, f32),
            pltpu.VMEM((cx, cy, cz), f32),
        ),
        in_specs=[hbm] * 7,
        out_specs=(vmem, vmem),
        scratch_shapes=[
            pltpu.SMEM(frequency.shape, f32),
            pltpu.SMEM(design_tiles.shape, jnp.int32),
            pltpu.SMEM(mix.shape, jnp.int32),
            pltpu.SMEM(pml_width.shape, jnp.int32),
        ]
        + [pltpu.VMEM(shape, f32) for shape in shapes]
        + [
            pltpu.SemaphoreType.DMA((2 + own,)),
            pltpu.SemaphoreType.DMA((HA + 1,)),
            pltpu.SemaphoreType.DMA((len(recv_slots(own)),)),
            pltpu.SemaphoreType.DMA((4,)),
            pltpu.SemaphoreType.DMA((4,)),
        ],
        compiler_params=pltpu.CompilerParams(collective_id=0, has_side_effects=True),
    )(
        forward_field,
        adjoint_source,
        permittivity,
        frequency,
        design_tiles,
        mix,
        pml_width,
    )
    return pl.pallas_call(
        store_kernel,
        out_shape=(
            jax.ShapeDtypeStruct(field, f32),
            jax.ShapeDtypeStruct((cx, cy, cz), f32),
        ),
        in_specs=[hbm, hbm],
        out_specs=(hbm, hbm),
        scratch_shapes=[pltpu.SemaphoreType.DMA((2,))],
        compiler_params=pltpu.CompilerParams(vmem_limit_bytes=1 << 20),
    )(adjoint, gradient)


def solution(mesh):
    return jax.shard_map(
        functools.partial(shards, mesh.shape["gx"], mesh.shape["gy"]),
        mesh=mesh,
        in_specs=(
            P("ha", None, None, ("cand", "gx"), "gy", None),
            P("ha", None, None, ("cand", "gx"), "gy", None),
            P(("cand", "gx"), "gy", None),
            P(),
            P(("cand", "gx"), "gy"),
            P(),
            P(),
        ),
        out_specs=(P("ha", None, None, ("cand", "gx"), "gy", None), P(("cand", "gx"), "gy", None)),
        check_vma=False,
    )
```

```python
import functools

import jax
import jax.numpy as jnp
from jax import lax
from jax.experimental import pallas as pl
from jax.experimental.pallas import tpu as pltpu
from jax.sharding import PartitionSpec as P

ITERS = 3
TILE = 4
PAIRS = 3

kerr_coef = 4.0
sigma_peak = 8.0

MESH = pl.DeviceIdType.MESH
XUP, XDN, YUP, YDN, CUP, CDN, HA = range(7)
YUP2, YDN2 = 12, 13
GRAIN = {XUP: 2, XDN: 2, YUP: 2, YDN: 2, CUP: 2, CDN: 2, HA: 1, YUP2: 2, YDN2: 2}


def cut(own, kind):
    cells = [(h, p) for h in range(own) for p in range(2)]
    size = len(cells) if GRAIN[kind] == 1 else 2
    return [cells[i : i + size] for i in range(0, len(cells), size)]


def recv_slots(own):
    messages = [(kind, s) for s in range(ITERS) for kind in range(7) if (kind, s) != (HA, 2)] + [(YUP2, 1), (YDN2, 1)]
    slots = [(kind, s, u) for kind, s in messages for u in range(len(cut(own, kind)))]
    return {message: at for at, message in enumerate(slots)}


def kernel(
    size_x,
    size_y,
    fwd,
    src_hbm,
    perm_hbm,
    freq_hbm,
    tiles_hbm,
    mix_hbm,
    pml_hbm,
    out,
    gout,
    freq,
    tiles,
    mix,
    pml,
    fall,
    v0,
    v1,
    v2,
    src,
    perm,
    inv,
    gain,
    loss,
    kmask,
    held,
    part,
    other,
    xup_s,
    xup_r,
    xdn_r,
    yup_s,
    yup_r,
    ydn_s,
    ydn_r,
    cup_s,
    cup_r,
    cdn_s,
    cdn_r,
    load_sem,
    send_sem,
    recv_sem,
    fwd_sem,
    scalar_sem,
):
    own, _, _, cx, cy, cz = src.shape
    vs = (v0, v1, v2)
    gx = lax.axis_index("gx")
    gy = lax.axis_index("gy")
    ha = lax.axis_index("ha")
    has_xm, has_xp = gx > 0, gx < size_x - 1
    has_ym, has_yp = gy > 0, gy < size_y - 1
    xm, xp = jnp.maximum(gx - 1, 0), jnp.minimum(gx + 1, size_x - 1)
    ym, yp = jnp.maximum(gy - 1, 0), jnp.minimum(gy + 1, size_y - 1)
    mate = {"ha": 1 - ha}
    mine, theirs = ha * own, (1 - ha) * own
    made = (mine, theirs, theirs)
    work = (theirs, theirs, mine)

    load_scalars = [
        pltpu.make_async_copy(source, target, scalar_sem.at[i])
        for i, (source, target) in enumerate(
            ((freq_hbm, freq), (pml_hbm, pml), (tiles_hbm, tiles), (mix_hbm, mix))
        )
    ]
    load_perm = pltpu.make_async_copy(perm_hbm, perm, load_sem.at[0])
    load_src = [
        pltpu.make_async_copy(src_hbm.at[h], src.at[h], load_sem.at[1 + h]) for h in range(own)
    ]
    load_fwd = pltpu.make_async_copy(fwd, fall.at[pl.ds(mine, own)], load_sem.at[1 + own])

    barrier = pltpu.get_barrier_semaphore()
    peers = (
        (has_xp, {"gx": xp}),
        (has_xm, {"gx": xm}),
        (has_yp, {"gy": yp}),
        (has_ym, {"gy": ym}),
        (has_xp & has_ym, {"gx": xp, "gy": ym}),
        (has_xm & has_yp, {"gx": xm, "gy": yp}),
    )
    pl.semaphore_signal(barrier, inc=1, device_id=mate, device_id_type=MESH)
    count = jnp.int32(1)
    for there, peer in peers:
        count = count + there.astype(jnp.int32)

        @pl.when(there)
        def _():
            pl.semaphore_signal(barrier, inc=1, device_id=peer | mate, device_id_type=MESH)

    load_scalars[0].start()
    load_perm.start()
    for copy in load_src:
        copy.start()
    for copy in load_scalars[1:]:
        copy.start()
    load_fwd.start()

    units = cut(own, XUP)
    slots = recv_slots(own)
    every, low, high = pl.ds(0, cx), pl.ds(0, cx - 1), pl.ds(cx - 1, 1)
    low_up, high_up = pl.ds(0, cx - 2), pl.ds(cx - 2, 2)

    def which(kind, u, base=0):
        h, _ = cut(own, kind)[u][0]
        return (base + h if GRAIN[kind] == 2 else pl.ds(base, own)), slice(None)

    def spot(ref, s, kind, u, rows=None):
        return ref.at[(s,) + which(kind, u) + (() if rows is None else (rows,))]

    def block(v, kind, base, u, tail):
        return v.at[which(kind, u, base) + tail]

    def link(kind, s, u):
        v = vs[s]
        to = mate if work[s] is not made[s] else {}
        parted = s == 1
        first_up, first = (low_up, low) if parted else (every, every)
        if kind == HA:
            source = target = block(v, HA, made[s], u, (slice(None),))
            peer, sends, gets = mate, None, None
        else:
            face, halo, rows, peer, sends, gets = {
                XUP: (xup_s, xup_r, None, {"gx": xp}, has_xp, has_xm),
                XDN: (None, xdn_r, None, {"gx": xm}, has_xm, has_xp),
                YUP: (yup_s, yup_r, first_up, {"gy": yp}, has_yp, has_ym),
                YDN: (ydn_s, ydn_r, first, {"gy": ym}, has_ym, has_yp),
                YUP2: (yup_s, yup_r, high_up, {"gy": yp}, has_yp, has_ym),
                YDN2: (ydn_s, ydn_r, high, {"gy": ym}, has_ym, has_yp),
                CUP: (cup_s, cup_r, None, {"gx": xp, "gy": ym}, has_xp & has_ym, has_xm & has_yp),
                CDN: (cdn_s, cdn_r, None, {"gx": xm, "gy": yp}, has_xm & has_yp, has_xp & has_ym),
            }[kind]
            peer = peer | to
            target = spot(halo, s, kind, u, rows)
            if kind == XDN:
                source = block(v, XDN, made[s], u, (pl.ds(1, 2), 0))
            else:
                source = spot(face, s, kind, u, rows)
        copy = pltpu.make_async_remote_copy(
            src_ref=source,
            dst_ref=target,
            send_sem=send_sem.at[kind % 10],
            recv_sem=recv_sem.at[slots[kind, s % 2 if kind == HA else s, u]],
            device_id=peer,
            device_id_type=MESH,
        )
        return copy, sends, gets

    def send(kind, s, u):
        copy, sends, _ = link(kind, s, u)
        if sends is None:
            copy.start()
        else:
            pl.when(sends)(copy.start)

    def all_sent():
        for kind, halo in enumerate((xup_r, xdn_r, yup_r, ydn_r, cup_r, cdn_r)):
            copy, sends, _ = link(kind, 0, 0)
            total = pltpu.make_async_remote_copy(
                src_ref=halo,
                dst_ref=halo,
                send_sem=send_sem.at[kind],
                recv_sem=recv_sem.at[0],
                device_id=mate,
                device_id_type=MESH,
            )
            pl.when(sends)(total.wait_send)

    def mate_has(s):
        total = vs[s].at[pl.ds(made[s], own)]
        pltpu.make_async_remote_copy(
            src_ref=total,
            dst_ref=total,
            send_sem=send_sem.at[HA],
            recv_sem=recv_sem.at[0],
            device_id=mate,
            device_id_type=MESH,
        ).wait_send()

    def arrived(kind, s, u):
        if kind == HA:
            place = block(vs[s], HA, own - made[s], u, (slice(None),))
            pltpu.make_async_remote_copy(
                src_ref=place,
                dst_ref=place,
                send_sem=send_sem.at[HA],
                recv_sem=recv_sem.at[slots[kind, s % 2 if kind == HA else s, u]],
                device_id=mate,
                device_id_type=MESH,
            ).wait_recv()
        else:
            copy, _, gets = link(kind, s, u)
            pl.when(gets)(copy.wait_recv)

    iy = lax.broadcasted_iota(jnp.int32, (cy, cz), 0)
    iz = lax.broadcasted_iota(jnp.int32, (cy, cz), 1)
    keep_x = has_xm.astype(jnp.float32)
    keep_y = has_ym.astype(jnp.float32)

    def z_ahead(f):
        return jnp.where(iz == cz - 1, 0.0, pltpu.roll(f, cz - 1, 1))

    def z_behind(f):
        return jnp.where(iz == 0, 0.0, pltpu.roll(f, 1, 1))

    def y_ahead(f, row):
        return jnp.where(iy == cy - 1, row, pltpu.roll(f, cy - 1, 0))

    def y_behind(f, row):
        return jnp.where(iy == 0, row, pltpu.roll(f, 1, 0))

    def profile(width, extent, place):
        reach = jnp.maximum(jnp.maximum(width - place, place - (extent - 1 - width)), 0)
        ratio = reach.astype(jnp.float32) / jnp.full((cy, cz), width).astype(jnp.float32)
        return ratio * ratio

    def pack_up(s, h, p, f):
        fx, fy, fz = (f(c, cx - 1) for c in range(3))
        cup_s[s, h, p] = fx[0:1]
        xup_s[s, h, p, 0] = fy + y_ahead(fx, 0.0) - fx
        xup_s[s, h, p, 1] = fz + z_ahead(fx) - fx

    def pack_down(s, h, p, f):
        cdn_s[s, h, p] = f(1, 0)[cy - 1 : cy]

    def pack_y(s, h, p, f, up, down):
        for x in up:
            fx, fy, fz = (f(c, x)[cy - 1 : cy] for c in range(3))
            ahead = f(1, x + 1)[cy - 1 : cy] if x < cx - 1 else 0.0
            row_z = jnp.where(iz[0:1] == cz - 1, 0.0, pltpu.roll(fy, cz - 1, 1))
            yup_s[s, h, p, x, 0:1, :] = fx + ahead - fy
            yup_s[s, h, p, x, 1:2, :] = fz + row_z - fy
        for x in down:
            ydn_s[s, h, p, x, 0:1, :] = f(0, x)[0:1]
            ydn_s[s, h, p, x, 1:2, :] = f(2, x)[0:1]

    def send_all(s, kinds, unit):
        for kind in kinds:
            for u, cells in enumerate(cut(own, kind)):
                if cells[-1] in unit:
                    send(kind, s, u)

    load_scalars[0].wait()
    squared = [freq[i] * freq[i] for i in range(2 * own)]
    squared_mine = [freq[mine + h] * freq[mine + h] for h in range(own)]
    load_perm.wait()
    scales = {}
    for h in range(own):
        for x in range(cx):
            scales[h, x] = 1.0 / (10.0 + squared_mine[h] * perm[x])
    for h in range(own):
        load_src[h].wait()
        for p in range(2):
            f = {}
            for x in range(cx):
                for c in range(3):
                    f[c, x] = src[h, p, c, x] * scales[h, x]
                    v0[mine + h, p, c, x] = f[c, x]
            take = lambda c, x: f[c, x]
            pack_up(0, h, p, take)
            pack_down(0, h, p, take)
            pack_y(0, h, p, take, range(cx), range(cx))

    pl.semaphore_wait(barrier, count)
    for unit in units:
        send_all(0, (CUP, CDN, XUP, XDN, YUP, YDN), unit)
    for unit in units:
        send_all(0, (HA,), unit)
    fwd_copy = pltpu.make_async_remote_copy(
        src_ref=fwd,
        dst_ref=fall.at[pl.ds(mine, own)],
        send_sem=fwd_sem.at[0],
        recv_sem=fwd_sem.at[1],
        device_id=mate,
        device_id_type=MESH,
    )
    fwd_copy.start()

    for there, halo in (
        (has_xm, xup_r),
        (has_xp, xdn_r),
        (has_ym, yup_r),
        (has_yp, ydn_r),
        (has_xm & has_yp, cup_r),
        (has_xp & has_ym, cdn_r),
    ):

        @pl.when(jnp.logical_not(there))
        def _():
            halo[...] = jnp.zeros_like(halo)

    for copy in load_scalars[1:]:
        copy.wait()
    sigma_yz = profile(pml[1], cy * size_y, gy * cy + iy) + profile(pml[2], cz, iz)
    masks = []
    for x in range(cx):
        place = jnp.full((cy, cz), gx * cx + x)
        sigma = sigma_peak * (profile(pml[0], cx * size_x, place) + sigma_yz)
        mask = jnp.zeros((cy, cz), jnp.float32)
        for t in range(cy // TILE):
            inside = (iy >= t * TILE) & (iy < (t + 1) * TILE)
            mask = jnp.where(inside, tiles[x // TILE, t].astype(jnp.float32), mask)
        for i in range(2 * own):
            weighed = squared[i] * perm[x]
            inv[i, x] = 1.0 / (10.0 + weighed)
            gain[i, x] = 10.0 + 2.0 * weighed
            loss[i, x] = squared[i] * sigma
            kmask[i, x] = (kerr_coef * squared[i]) * mask
        masks.append(mask)

    def fwd_arrived():
        load_fwd.wait()
        pltpu.make_async_remote_copy(
            src_ref=fwd,
            dst_ref=fall.at[pl.ds(theirs, own)],
            send_sem=fwd_sem.at[0],
            recv_sem=fwd_sem.at[1],
            device_id=mate,
            device_id_type=MESH,
        ).wait_recv()

    grads = {}

    def local(s, planes):
        v = vs[s]
        base = work[s]
        for h in range(own):
            gh = base + h
            for p in range(2):
                field = lambda c, x: v[gh, p, c, x]
                mz_behind = my_behind = None
                for x in planes:
                    fx, fy, fz = field(0, x), field(1, x), field(2, x)
                    fy_ahead = field(1, x + 1) if x < cx - 1 else 0.0
                    fz_ahead = field(2, x + 1) if x < cx - 1 else 0.0
                    mx = (y_ahead(fz, 0.0) - fz) - (z_ahead(fy) - fy)
                    my = (z_ahead(fx) - fx) - (fz_ahead - fz)
                    mz = (fy_ahead - fy) - (y_ahead(fx, 0.0) - fx)
                    if x == 0:
                        mz_behind, my_behind = keep_x * fy, -keep_x * fz
                    elif mz_behind is None:
                        bx, by, bz = (field(c, x - 1) for c in range(3))
                        my_behind = (z_ahead(bx) - bx) - (fz - bz)
                        mz_behind = (fy - by) - (y_ahead(bx, 0.0) - bx)
                    mz_low = y_behind(mz, -keep_y * fx)
                    mx_low = y_behind(mx, keep_y * fz)
                    curls = (
                        (mz - mz_low) - (my - z_behind(my)),
                        (mx - z_behind(mx)) - (mz - mz_behind),
                        (my - my_behind) - (mx - mx_low),
                    )
                    my_behind, mz_behind = my, mz
                    k1, k2 = gain[gh, x], loss[gh, x]
                    scale = 0.5 * k1 + 5.0
                    for c, at_c in enumerate((fx, fy, fz)):
                        turned = k2 * v[gh, 1 - p, c, x]
                        turned = -turned if p == 0 else turned
                        given = src[h, p, c, x] if base is mine else v0[gh, p, c, x] * scale
                        held[h, p, c, x] = given + k1 * at_c + turned - curls[c]

    def mixed(s, planes):
        v = vs[s]
        base = work[s]
        for h in range(own):
            firsts = [mix[k, 0, base + h] for k in range(PAIRS)]
            seconds = [mix[k, 1, base + h] for k in range(PAIRS)]
            for x in planes:
                k3 = kmask[base + h, x]
                for c in range(3):
                    real = imag = None
                    for a, b in zip(firsts, seconds):
                        fr, fi = fall[a, 0, c, x], fall[a, 1, c, x]
                        vr, vi = v[b, 0, c, x], v[b, 1, c, x]
                        re, im = fr * vr - fi * vi, fr * vi + fi * vr
                        real = re if real is None else real + re
                        imag = im if imag is None else imag + im
                    held[h, 0, c, x] = held[h, 0, c, x] + k3 * real
                    held[h, 1, c, x] = held[h, 1, c, x] + k3 * imag

    def finish(s, h, p, planes):
        gh = work[s] + h
        f = {}
        for x in planes:
            scale = inv[gh, x]
            row = lambda ref, c, at: ref[s, h, p, at, c : c + 1, :]
            fx_next, fz_next = row(ydn_r, 0, x), row(ydn_r, 1, x)
            low_z, low_x = row(yup_r, 0, x), row(yup_r, 1, x)
            if x == cx - 1:
                low_z = low_z + cdn_r[s, h, p]
            fx_prev = row(ydn_r, 0, x - 1) if x > 0 else cup_r[s, h, p]
            fz_step = fz_next - jnp.where(iz[0:1] == 0, 0.0, pltpu.roll(fz_next, 1, 1))
            less_x = jnp.where(iy == 0, low_z, jnp.where(iy == cy - 1, fx_next, 0.0))
            less_y = jnp.where(iy == cy - 1, fx_prev - fx_next - fz_step, 0.0)
            less_z = jnp.where(iy == 0, low_x, jnp.where(iy == cy - 1, fz_next, 0.0))
            if x == 0:
                less_y = less_y + xup_r[s, h, p, 0]
                less_z = less_z + xup_r[s, h, p, 1]
            if x == cx - 1:
                fy_ahead, fz_ahead = xdn_r[s, h, p, 0], xdn_r[s, h, p, 1]
                steps = (fy_ahead - y_behind(fy_ahead, 0.0)) + (fz_ahead - z_behind(fz_ahead))
                less_x = less_x - steps
                less_y = less_y + fy_ahead
                less_z = less_z + fz_ahead
            total = None
            for c, less in enumerate((less_x, less_y, less_z)):
                new = scale * (held[h, p, c, x] + less)
                f[c, x] = new
                if s < ITERS - 1:
                    vs[s + 1][gh, p, c, x] = new
                else:
                    out[h, p, c, x] = new
                    term = new * fall[gh, p, c, x]
                    total = term if total is None else total + term
            if s == ITERS - 1:
                total = (squared_mine[h] if p == 0 else -squared_mine[h]) * total
                grads[x] = grads[x] + total if x in grads else total
        if s == ITERS - 1:
            return None
        v = vs[s + 1]
        return lambda c, x: f[c, x] if (c, x) in f else v[gh, p, c, x]

    def stage(s, waits, planes, steps):
        for unit in units:
            for kind in waits:
                for u, cells in enumerate(cut(own, kind)):
                    if cells[0] in unit:
                        arrived(kind, s, u)
            fields = [(h, p, finish(s, h, p, planes)) for h, p in unit]
            for pack, kinds in steps:
                for h, p, f in fields:
                    if pack is not None:
                        pack(s + 1, h, p, f)
                send_all(s + 1, kinds, unit)

    def wait_all(kind, s):
        for u in range(len(cut(own, kind))):
            arrived(kind, s, u)

    def pack_y_low(s, h, p, f):
        pack_y(s, h, p, f, range(cx - 2), range(cx - 1))

    def pack_y_high(s, h, p, f):
        pack_y(s, h, p, f, range(cx - 2, cx), [cx - 1])

    shared = []

    def share(at, first, size):
        for x in range(first, first + size):
            part[x] = masks[x] * grads[x]
        copy = pltpu.make_async_remote_copy(
            src_ref=part.at[pl.ds(first, size)],
            dst_ref=other.at[pl.ds(first, size)],
            send_sem=fwd_sem.at[2 * at],
            recv_sem=fwd_sem.at[2 * at + 1],
            device_id=mate,
            device_id_type=MESH,
        )
        copy.start()
        shared.append(copy)

    planes, inner = range(cx), range(1, cx - 1)
    wait_all(HA, 0)
    local(0, planes)
    fwd_arrived()
    mixed(0, planes)
    stage(0, (XUP, CUP, YUP, YDN), [0], [(pack_down, (CDN, XDN))])
    stage(0, (), inner, [(pack_y_low, (YUP, YDN))])
    stage(0, (XDN, CDN), [cx - 1], [(pack_up, (CUP, XUP)), (pack_y_high, (YUP2, YDN2))])
    mate_has(0)
    for unit in units:
        send_all(1, (HA,), unit)
    local(1, planes)
    wait_all(HA, 1)
    mixed(1, planes)
    stage(1, (XUP, CUP, YUP, YDN), [0], [(pack_down, (CDN, XDN))])
    stage(1, (YUP2, YDN2), inner, [(pack_y_low, ())])
    stage(1, (XDN, CDN), [cx - 1], [(pack_up, (CUP, XUP)), (pack_y_high, (YUP, YDN))])
    mate_has(1)
    for unit in units:
        send_all(2, (HA,), unit)
    fwd_copy.wait_send()
    wait_all(HA, 2)
    local(2, planes)
    mixed(2, planes)
    stage(2, (XUP, CUP, YUP, YDN), range(cx - 1), [])
    share(0, 0, cx - 1)
    stage(2, (XDN, CDN), [cx - 1], [])
    mate_has(2)

    share(1, cx - 1, 1)
    all_sent()
    for copy in shared:
        copy.wait()
    gout[...] = part[...] + other[...]


def store_kernel(adjoint, gradient, out, gout, sem):
    copies = [
        pltpu.make_async_copy(adjoint, out, sem.at[0]),
        pltpu.make_async_copy(gradient, gout, sem.at[1]),
    ]
    for copy in copies:
        copy.start()
    for copy in copies:
        copy.wait()


def shards(
    size_x,
    size_y,
    forward_field,
    adjoint_source,
    permittivity,
    frequency,
    design_tiles,
    mix_pairs,
    pml_width,
):
    own = forward_field.shape[0]
    cx, cy, cz = permittivity.shape
    f32 = jnp.float32
    field = forward_field.shape
    everyone = (2 * own,) + field[1:]
    planes = (2 * own, cx, cy, cz)
    face_x = (ITERS, own, 2, 2, cy, cz)
    face_y = (ITERS, own, 2, cx, 2, cz)
    edge = (ITERS, own, 2, 1, cz)
    hbm = pl.BlockSpec(memory_space=pl.ANY)
    vmem = pl.BlockSpec(memory_space=pltpu.VMEM)
    mix = jnp.transpose(mix_pairs, (1, 2, 0))
    shapes = (
        [everyone] * 4
        + [field, (cx, cy, cz)]
        + [planes] * 4
        + [field, (cx, cy, cz), (cx, cy, cz)]
        + [face_x] * 3
        + [face_y] * 4
        + [edge] * 4
    )
    adjoint, gradient = pl.pallas_call(
        functools.partial(kernel, size_x, size_y),
        out_shape=(
            pltpu.VMEM(field, f32),
            pltpu.VMEM((cx, cy, cz), f32),
        ),
        in_specs=[hbm] * 7,
        out_specs=(vmem, vmem),
        scratch_shapes=[
            pltpu.SMEM(frequency.shape, f32),
            pltpu.SMEM(design_tiles.shape, jnp.int32),
            pltpu.SMEM(mix.shape, jnp.int32),
            pltpu.SMEM(pml_width.shape, jnp.int32),
        ]
        + [pltpu.VMEM(shape, f32) for shape in shapes]
        + [
            pltpu.SemaphoreType.DMA((2 + own,)),
            pltpu.SemaphoreType.DMA((HA + 1,)),
            pltpu.SemaphoreType.DMA((len(recv_slots(own)),)),
            pltpu.SemaphoreType.DMA((4,)),
            pltpu.SemaphoreType.DMA((4,)),
        ],
        compiler_params=pltpu.CompilerParams(collective_id=0, has_side_effects=True),
    )(
        forward_field,
        adjoint_source,
        permittivity,
        frequency,
        design_tiles,
        mix,
        pml_width,
    )
    return pl.pallas_call(
        store_kernel,
        out_shape=(
            jax.ShapeDtypeStruct(field, f32),
            jax.ShapeDtypeStruct((cx, cy, cz), f32),
        ),
        in_specs=[hbm, hbm],
        out_specs=(hbm, hbm),
        scratch_shapes=[pltpu.SemaphoreType.DMA((2,))],
        compiler_params=pltpu.CompilerParams(vmem_limit_bytes=1 << 20),
    )(adjoint, gradient)


def solution(mesh):
    return jax.shard_map(
        functools.partial(shards, mesh.shape["gx"], mesh.shape["gy"]),
        mesh=mesh,
        in_specs=(
            P("ha", None, None, ("cand", "gx"), "gy", None),
            P("ha", None, None, ("cand", "gx"), "gy", None),
            P(("cand", "gx"), "gy", None),
            P(),
            P(("cand", "gx"), "gy"),
            P(),
            P(),
        ),
        out_specs=(P("ha", None, None, ("cand", "gx"), "gy", None), P(("cand", "gx"), "gy", None)),
        check_vma=False,
    )
```

```python
import functools

import jax
import jax.numpy as jnp
from jax import lax
from jax.experimental import pallas as pl
from jax.experimental.pallas import tpu as pltpu
from jax.sharding import PartitionSpec as P

ITERS = 3
TILE = 4
PAIRS = 3

kerr_coef = 4.0
sigma_peak = 8.0

MESH = pl.DeviceIdType.MESH
XUP, XDN, YUP, YDN, CUP, CDN, HA = range(7)
YUP2, YDN2 = 12, 13
GRAIN = {XUP: 2, XDN: 2, YUP: 2, YDN: 2, CUP: 2, CDN: 2, HA: 1, YUP2: 2, YDN2: 2}


def cut(own, kind):
    cells = [(h, p) for h in range(own) for p in range(2)]
    size = len(cells) if GRAIN[kind] == 1 else 2
    return [cells[i : i + size] for i in range(0, len(cells), size)]


def recv_slots(own):
    messages = [(kind, s) for s in range(ITERS) for kind in range(7) if (kind, s) != (HA, 2)] + [(YUP2, 1), (YDN2, 1)]
    slots = [(kind, s, u) for kind, s in messages for u in range(len(cut(own, kind)))]
    return {message: at for at, message in enumerate(slots)}


def kernel(
    size_x,
    size_y,
    fwd,
    src_hbm,
    perm_hbm,
    freq_hbm,
    tiles_hbm,
    mix_hbm,
    pml_hbm,
    out,
    gout,
    freq,
    tiles,
    mix,
    pml,
    fall,
    v0,
    v1,
    v2,
    src,
    perm,
    inv,
    gain,
    loss,
    kmask,
    held,
    part,
    other,
    xup_s,
    xup_r,
    xdn_r,
    yup_s,
    yup_r,
    ydn_s,
    ydn_r,
    cup_s,
    cup_r,
    cdn_s,
    cdn_r,
    load_sem,
    send_sem,
    recv_sem,
    fwd_sem,
    scalar_sem,
):
    own, _, _, cx, cy, cz = src.shape
    vs = (v0, v1, v2)
    gx = lax.axis_index("gx")
    gy = lax.axis_index("gy")
    ha = lax.axis_index("ha")
    has_xm, has_xp = gx > 0, gx < size_x - 1
    has_ym, has_yp = gy > 0, gy < size_y - 1
    xm, xp = jnp.maximum(gx - 1, 0), jnp.minimum(gx + 1, size_x - 1)
    ym, yp = jnp.maximum(gy - 1, 0), jnp.minimum(gy + 1, size_y - 1)
    mate = {"ha": 1 - ha}
    mine, theirs = ha * own, (1 - ha) * own
    made = (mine, theirs, theirs)
    work = (theirs, theirs, mine)

    load_scalars = [
        pltpu.make_async_copy(source, target, scalar_sem.at[i])
        for i, (source, target) in enumerate(
            ((freq_hbm, freq), (pml_hbm, pml), (tiles_hbm, tiles), (mix_hbm, mix))
        )
    ]
    load_perm = pltpu.make_async_copy(perm_hbm, perm, load_sem.at[0])
    load_src = [
        pltpu.make_async_copy(src_hbm.at[h], src.at[h], load_sem.at[1 + h]) for h in range(own)
    ]
    load_fwd = pltpu.make_async_copy(fwd, fall.at[pl.ds(mine, own)], load_sem.at[1 + own])

    barrier = pltpu.get_barrier_semaphore()
    peers = (
        (has_xp, {"gx": xp}),
        (has_xm, {"gx": xm}),
        (has_yp, {"gy": yp}),
        (has_ym, {"gy": ym}),
        (has_xp & has_ym, {"gx": xp, "gy": ym}),
        (has_xm & has_yp, {"gx": xm, "gy": yp}),
    )
    pl.semaphore_signal(barrier, inc=1, device_id=mate, device_id_type=MESH)
    count = jnp.int32(1)
    for there, peer in peers:
        count = count + there.astype(jnp.int32)

        @pl.when(there)
        def _():
            pl.semaphore_signal(barrier, inc=1, device_id=peer | mate, device_id_type=MESH)

    load_scalars[0].start()
    load_perm.start()
    for copy in load_src:
        copy.start()
    for copy in load_scalars[1:]:
        copy.start()
    load_fwd.start()

    units = cut(own, XUP)
    slots = recv_slots(own)
    every, low, high = pl.ds(0, cx), pl.ds(0, cx - 1), pl.ds(cx - 1, 1)
    low_up, high_up = pl.ds(0, cx - 2), pl.ds(cx - 2, 2)

    def which(kind, u, base=0):
        h, _ = cut(own, kind)[u][0]
        return (base + h if GRAIN[kind] == 2 else pl.ds(base, own)), slice(None)

    def spot(ref, s, kind, u, rows=None):
        return ref.at[(s,) + which(kind, u) + (() if rows is None else (rows,))]

    def block(v, kind, base, u, tail):
        return v.at[which(kind, u, base) + tail]

    def link(kind, s, u):
        v = vs[s]
        to = mate if work[s] is not made[s] else {}
        parted = s == 1
        first_up, first = (low_up, low) if parted else (every, every)
        if kind == HA:
            source = target = block(v, HA, made[s], u, (slice(None),))
            peer, sends, gets = mate, None, None
        else:
            face, halo, rows, peer, sends, gets = {
                XUP: (xup_s, xup_r, None, {"gx": xp}, has_xp, has_xm),
                XDN: (None, xdn_r, None, {"gx": xm}, has_xm, has_xp),
                YUP: (yup_s, yup_r, first_up, {"gy": yp}, has_yp, has_ym),
                YDN: (ydn_s, ydn_r, first, {"gy": ym}, has_ym, has_yp),
                YUP2: (yup_s, yup_r, high_up, {"gy": yp}, has_yp, has_ym),
                YDN2: (ydn_s, ydn_r, high, {"gy": ym}, has_ym, has_yp),
                CUP: (cup_s, cup_r, None, {"gx": xp, "gy": ym}, has_xp & has_ym, has_xm & has_yp),
                CDN: (cdn_s, cdn_r, None, {"gx": xm, "gy": yp}, has_xm & has_yp, has_xp & has_ym),
            }[kind]
            peer = peer | to
            target = spot(halo, s, kind, u, rows)
            if kind == XDN:
                source = block(v, XDN, made[s], u, (pl.ds(1, 2), 0))
            else:
                source = spot(face, s, kind, u, rows)
        copy = pltpu.make_async_remote_copy(
            src_ref=source,
            dst_ref=target,
            send_sem=send_sem.at[kind % 10],
            recv_sem=recv_sem.at[slots[kind, s % 2 if kind == HA else s, u]],
            device_id=peer,
            device_id_type=MESH,
        )
        return copy, sends, gets

    def send(kind, s, u):
        copy, sends, _ = link(kind, s, u)
        if sends is None:
            copy.start()
        else:
            pl.when(sends)(copy.start)

    def all_sent():
        for kind, halo in enumerate((xup_r, xdn_r, yup_r, ydn_r, cup_r, cdn_r)):
            copy, sends, _ = link(kind, 0, 0)
            total = pltpu.make_async_remote_copy(
                src_ref=halo,
                dst_ref=halo,
                send_sem=send_sem.at[kind],
                recv_sem=recv_sem.at[0],
                device_id=mate,
                device_id_type=MESH,
            )
            pl.when(sends)(total.wait_send)

    def mate_has(s):
        total = vs[s].at[pl.ds(made[s], own)]
        pltpu.make_async_remote_copy(
            src_ref=total,
            dst_ref=total,
            send_sem=send_sem.at[HA],
            recv_sem=recv_sem.at[0],
            device_id=mate,
            device_id_type=MESH,
        ).wait_send()

    def arrived(kind, s, u):
        if kind == HA:
            place = block(vs[s], HA, own - made[s], u, (slice(None),))
            pltpu.make_async_remote_copy(
                src_ref=place,
                dst_ref=place,
                send_sem=send_sem.at[HA],
                recv_sem=recv_sem.at[slots[kind, s % 2 if kind == HA else s, u]],
                device_id=mate,
                device_id_type=MESH,
            ).wait_recv()
        else:
            copy, _, gets = link(kind, s, u)
            pl.when(gets)(copy.wait_recv)

    iy = lax.broadcasted_iota(jnp.int32, (cy, cz), 0)
    iz = lax.broadcasted_iota(jnp.int32, (cy, cz), 1)
    keep_x = has_xm.astype(jnp.float32)
    keep_y = has_ym.astype(jnp.float32)

    def z_ahead(f):
        return jnp.where(iz == cz - 1, 0.0, pltpu.roll(f, cz - 1, 1))

    def z_behind(f):
        return jnp.where(iz == 0, 0.0, pltpu.roll(f, 1, 1))

    def y_ahead(f, row):
        return jnp.where(iy == cy - 1, row, pltpu.roll(f, cy - 1, 0))

    def y_behind(f, row):
        return jnp.where(iy == 0, row, pltpu.roll(f, 1, 0))

    def profile(width, extent, place):
        reach = jnp.maximum(jnp.maximum(width - place, place - (extent - 1 - width)), 0)
        ratio = reach.astype(jnp.float32) / jnp.full((cy, cz), width).astype(jnp.float32)
        return ratio * ratio

    def pack_up(s, h, p, f):
        fx, fy, fz = (f(c, cx - 1) for c in range(3))
        cup_s[s, h, p] = fx[0:1]
        xup_s[s, h, p, 0] = fy + y_ahead(fx, 0.0) - fx
        xup_s[s, h, p, 1] = fz + z_ahead(fx) - fx

    def pack_down(s, h, p, f):
        cdn_s[s, h, p] = f(1, 0)[cy - 1 : cy]

    def pack_y(s, h, p, f, up, down):
        for x in up:
            fx, fy, fz = (f(c, x)[cy - 1 : cy] for c in range(3))
            ahead = f(1, x + 1)[cy - 1 : cy] if x < cx - 1 else 0.0
            row_z = jnp.where(iz[0:1] == cz - 1, 0.0, pltpu.roll(fy, cz - 1, 1))
            yup_s[s, h, p, x, 0:1, :] = fx + ahead - fy
            yup_s[s, h, p, x, 1:2, :] = fz + row_z - fy
        for x in down:
            ydn_s[s, h, p, x, 0:1, :] = f(0, x)[0:1]
            ydn_s[s, h, p, x, 1:2, :] = f(2, x)[0:1]

    def send_all(s, kinds, unit):
        for kind in kinds:
            for u, cells in enumerate(cut(own, kind)):
                if cells[-1] in unit:
                    send(kind, s, u)

    load_scalars[0].wait()
    squared = [freq[i] * freq[i] for i in range(2 * own)]
    squared_mine = [freq[mine + h] * freq[mine + h] for h in range(own)]
    load_perm.wait()
    scales = {}
    for h in range(own):
        for x in range(cx):
            scales[h, x] = 1.0 / (10.0 + squared_mine[h] * perm[x])
    for h in range(own):
        load_src[h].wait()
        for p in range(2):
            f = {}
            for x in range(cx):
                for c in range(3):
                    f[c, x] = src[h, p, c, x] * scales[h, x]
                    v0[mine + h, p, c, x] = f[c, x]
            take = lambda c, x: f[c, x]
            pack_up(0, h, p, take)
            pack_down(0, h, p, take)
            pack_y(0, h, p, take, range(cx), range(cx))

    pl.semaphore_wait(barrier, count)
    for unit in units:
        send_all(0, (XDN, XUP, CDN, CUP, YDN, YUP), unit)
    fwd_copy = pltpu.make_async_remote_copy(
        src_ref=fwd,
        dst_ref=fall.at[pl.ds(mine, own)],
        send_sem=fwd_sem.at[0],
        recv_sem=fwd_sem.at[1],
        device_id=mate,
        device_id_type=MESH,
    )
    fwd_copy.start()
    for unit in units:
        send_all(0, (HA,), unit)

    for there, halo in (
        (has_xm, xup_r),
        (has_xp, xdn_r),
        (has_ym, yup_r),
        (has_yp, ydn_r),
        (has_xm & has_yp, cup_r),
        (has_xp & has_ym, cdn_r),
    ):

        @pl.when(jnp.logical_not(there))
        def _():
            halo[...] = jnp.zeros_like(halo)

    for copy in load_scalars[1:]:
        copy.wait()
    sigma_yz = profile(pml[1], cy * size_y, gy * cy + iy) + profile(pml[2], cz, iz)
    masks = []
    for x in range(cx):
        place = jnp.full((cy, cz), gx * cx + x)
        sigma = sigma_peak * (profile(pml[0], cx * size_x, place) + sigma_yz)
        mask = jnp.zeros((cy, cz), jnp.float32)
        for t in range(cy // TILE):
            inside = (iy >= t * TILE) & (iy < (t + 1) * TILE)
            mask = jnp.where(inside, tiles[x // TILE, t].astype(jnp.float32), mask)
        for i in range(2 * own):
            weighed = squared[i] * perm[x]
            inv[i, x] = 1.0 / (10.0 + weighed)
            gain[i, x] = 10.0 + 2.0 * weighed
            loss[i, x] = squared[i] * sigma
            kmask[i, x] = (kerr_coef * squared[i]) * mask
        masks.append(mask)

    def fwd_arrived():
        load_fwd.wait()
        pltpu.make_async_remote_copy(
            src_ref=fwd,
            dst_ref=fall.at[pl.ds(theirs, own)],
            send_sem=fwd_sem.at[0],
            recv_sem=fwd_sem.at[1],
            device_id=mate,
            device_id_type=MESH,
        ).wait_recv()

    grads = {}

    def local(s, planes):
        v = vs[s]
        base = work[s]
        for h in range(own):
            gh = base + h
            for p in range(2):
                field = lambda c, x: v[gh, p, c, x]
                mz_behind = my_behind = None
                for x in planes:
                    fx, fy, fz = field(0, x), field(1, x), field(2, x)
                    fy_ahead = field(1, x + 1) if x < cx - 1 else 0.0
                    fz_ahead = field(2, x + 1) if x < cx - 1 else 0.0
                    mx = (y_ahead(fz, 0.0) - fz) - (z_ahead(fy) - fy)
                    my = (z_ahead(fx) - fx) - (fz_ahead - fz)
                    mz = (fy_ahead - fy) - (y_ahead(fx, 0.0) - fx)
                    if x == 0:
                        mz_behind, my_behind = keep_x * fy, -keep_x * fz
                    elif mz_behind is None:
                        bx, by, bz = (field(c, x - 1) for c in range(3))
                        my_behind = (z_ahead(bx) - bx) - (fz - bz)
                        mz_behind = (fy - by) - (y_ahead(bx, 0.0) - bx)
                    mz_low = y_behind(mz, -keep_y * fx)
                    mx_low = y_behind(mx, keep_y * fz)
                    curls = (
                        (mz - mz_low) - (my - z_behind(my)),
                        (mx - z_behind(mx)) - (mz - mz_behind),
                        (my - my_behind) - (mx - mx_low),
                    )
                    my_behind, mz_behind = my, mz
                    k1, k2 = gain[gh, x], loss[gh, x]
                    scale = 0.5 * k1 + 5.0
                    for c, at_c in enumerate((fx, fy, fz)):
                        turned = k2 * v[gh, 1 - p, c, x]
                        turned = -turned if p == 0 else turned
                        given = src[h, p, c, x] if base is mine else v0[gh, p, c, x] * scale
                        held[h, p, c, x] = given + k1 * at_c + turned - curls[c]

    def mixed(s, planes):
        v = vs[s]
        base = work[s]
        for h in range(own):
            firsts = [mix[k, 0, base + h] for k in range(PAIRS)]
            seconds = [mix[k, 1, base + h] for k in range(PAIRS)]
            for x in planes:
                k3 = kmask[base + h, x]
                for c in range(3):
                    real = imag = None
                    for a, b in zip(firsts, seconds):
                        fr, fi = fall[a, 0, c, x], fall[a, 1, c, x]
                        vr, vi = v[b, 0, c, x], v[b, 1, c, x]
                        re, im = fr * vr - fi * vi, fr * vi + fi * vr
                        real = re if real is None else real + re
                        imag = im if imag is None else imag + im
                    held[h, 0, c, x] = held[h, 0, c, x] + k3 * real
                    held[h, 1, c, x] = held[h, 1, c, x] + k3 * imag

    def finish(s, h, p, planes):
        gh = work[s] + h
        f = {}
        for x in planes:
            scale = inv[gh, x]
            row = lambda ref, c, at: ref[s, h, p, at, c : c + 1, :]
            fx_next, fz_next = row(ydn_r, 0, x), row(ydn_r, 1, x)
            low_z, low_x = row(yup_r, 0, x), row(yup_r, 1, x)
            if x == cx - 1:
                low_z = low_z + cdn_r[s, h, p]
            fx_prev = row(ydn_r, 0, x - 1) if x > 0 else cup_r[s, h, p]
            fz_step = fz_next - jnp.where(iz[0:1] == 0, 0.0, pltpu.roll(fz_next, 1, 1))
            less_x = jnp.where(iy == 0, low_z, jnp.where(iy == cy - 1, fx_next, 0.0))
            less_y = jnp.where(iy == cy - 1, fx_prev - fx_next - fz_step, 0.0)
            less_z = jnp.where(iy == 0, low_x, jnp.where(iy == cy - 1, fz_next, 0.0))
            if x == 0:
                less_y = less_y + xup_r[s, h, p, 0]
                less_z = less_z + xup_r[s, h, p, 1]
            if x == cx - 1:
                fy_ahead, fz_ahead = xdn_r[s, h, p, 0], xdn_r[s, h, p, 1]
                steps = (fy_ahead - y_behind(fy_ahead, 0.0)) + (fz_ahead - z_behind(fz_ahead))
                less_x = less_x - steps
                less_y = less_y + fy_ahead
                less_z = less_z + fz_ahead
            total = None
            for c, less in enumerate((less_x, less_y, less_z)):
                new = scale * (held[h, p, c, x] + less)
                f[c, x] = new
                if s < ITERS - 1:
                    vs[s + 1][gh, p, c, x] = new
                else:
                    out[h, p, c, x] = new
                    term = new * fall[gh, p, c, x]
                    total = term if total is None else total + term
            if s == ITERS - 1:
                total = (squared_mine[h] if p == 0 else -squared_mine[h]) * total
                grads[x] = grads[x] + total if x in grads else total
        if s == ITERS - 1:
            return None
        v = vs[s + 1]
        return lambda c, x: f[c, x] if (c, x) in f else v[gh, p, c, x]

    def stage(s, waits, planes, steps):
        for unit in units:
            for kind in waits:
                for u, cells in enumerate(cut(own, kind)):
                    if cells[0] in unit:
                        arrived(kind, s, u)
            fields = [(h, p, finish(s, h, p, planes)) for h, p in unit]
            for pack, kinds in steps:
                for h, p, f in fields:
                    if pack is not None:
                        pack(s + 1, h, p, f)
                send_all(s + 1, kinds, unit)

    def wait_all(kind, s):
        for u in range(len(cut(own, kind))):
            arrived(kind, s, u)

    def pack_y_low(s, h, p, f):
        pack_y(s, h, p, f, range(cx - 2), range(cx - 1))

    def pack_y_high(s, h, p, f):
        pack_y(s, h, p, f, range(cx - 2, cx), [cx - 1])

    shared = []

    def share(at, first, size):
        for x in range(first, first + size):
            part[x] = masks[x] * grads[x]
        copy = pltpu.make_async_remote_copy(
            src_ref=part.at[pl.ds(first, size)],
            dst_ref=other.at[pl.ds(first, size)],
            send_sem=fwd_sem.at[2 * at],
            recv_sem=fwd_sem.at[2 * at + 1],
            device_id=mate,
            device_id_type=MESH,
        )
        copy.start()
        shared.append(copy)

    planes, inner = range(cx), range(1, cx - 1)
    wait_all(HA, 0)
    local(0, planes)
    fwd_arrived()
    mixed(0, planes)
    stage(0, (XUP, CUP, YUP, YDN), [0], [(pack_down, (CDN, XDN))])
    stage(0, (), inner, [(pack_y_low, (YUP, YDN))])
    stage(0, (XDN, CDN), [cx - 1], [(pack_up, (CUP, XUP)), (pack_y_high, (YUP2, YDN2))])
    mate_has(0)
    for unit in units:
        send_all(1, (HA,), unit)
    local(1, planes)
    wait_all(HA, 1)
    mixed(1, planes)
    stage(1, (XUP, CUP, YUP, YDN), [0], [(pack_down, (CDN, XDN))])
    stage(1, (YUP2, YDN2), inner, [(pack_y_low, ())])
    stage(1, (XDN, CDN), [cx - 1], [(pack_up, (CUP, XUP)), (pack_y_high, (YUP, YDN))])
    mate_has(1)
    for unit in units:
        send_all(2, (HA,), unit)
    fwd_copy.wait_send()
    wait_all(HA, 2)
    local(2, planes)
    mixed(2, planes)
    stage(2, (XUP, CUP, YUP, YDN), range(cx - 1), [])
    share(0, 0, cx - 1)
    stage(2, (XDN, CDN), [cx - 1], [])
    mate_has(2)

    share(1, cx - 1, 1)
    all_sent()
    for copy in shared:
        copy.wait()
    gout[...] = part[...] + other[...]


def store_kernel(adjoint, gradient, out, gout, sem):
    copies = [
        pltpu.make_async_copy(adjoint, out, sem.at[0]),
        pltpu.make_async_copy(gradient, gout, sem.at[1]),
    ]
    for copy in copies:
        copy.start()
    for copy in copies:
        copy.wait()


def shards(
    size_x,
    size_y,
    forward_field,
    adjoint_source,
    permittivity,
    frequency,
    design_tiles,
    mix_pairs,
    pml_width,
):
    own = forward_field.shape[0]
    cx, cy, cz = permittivity.shape
    f32 = jnp.float32
    field = forward_field.shape
    everyone = (2 * own,) + field[1:]
    planes = (2 * own, cx, cy, cz)
    face_x = (ITERS, own, 2, 2, cy, cz)
    face_y = (ITERS, own, 2, cx, 2, cz)
    edge = (ITERS, own, 2, 1, cz)
    hbm = pl.BlockSpec(memory_space=pl.ANY)
    vmem = pl.BlockSpec(memory_space=pltpu.VMEM)
    mix = jnp.transpose(mix_pairs, (1, 2, 0))
    shapes = (
        [everyone] * 4
        + [field, (cx, cy, cz)]
        + [planes] * 4
        + [field, (cx, cy, cz), (cx, cy, cz)]
        + [face_x] * 3
        + [face_y] * 4
        + [edge] * 4
    )
    adjoint, gradient = pl.pallas_call(
        functools.partial(kernel, size_x, size_y),
        out_shape=(
            pltpu.VMEM(field, f32),
            pltpu.VMEM((cx, cy, cz), f32),
        ),
        in_specs=[hbm] * 7,
        out_specs=(vmem, vmem),
        scratch_shapes=[
            pltpu.SMEM(frequency.shape, f32),
            pltpu.SMEM(design_tiles.shape, jnp.int32),
            pltpu.SMEM(mix.shape, jnp.int32),
            pltpu.SMEM(pml_width.shape, jnp.int32),
        ]
        + [pltpu.VMEM(shape, f32) for shape in shapes]
        + [
            pltpu.SemaphoreType.DMA((2 + own,)),
            pltpu.SemaphoreType.DMA((HA + 1,)),
            pltpu.SemaphoreType.DMA((len(recv_slots(own)),)),
            pltpu.SemaphoreType.DMA((4,)),
            pltpu.SemaphoreType.DMA((4,)),
        ],
        compiler_params=pltpu.CompilerParams(collective_id=0, has_side_effects=True),
    )(
        forward_field,
        adjoint_source,
        permittivity,
        frequency,
        design_tiles,
        mix,
        pml_width,
    )
    return pl.pallas_call(
        store_kernel,
        out_shape=(
            jax.ShapeDtypeStruct(field, f32),
            jax.ShapeDtypeStruct((cx, cy, cz), f32),
        ),
        in_specs=[hbm, hbm],
        out_specs=(hbm, hbm),
        scratch_shapes=[pltpu.SemaphoreType.DMA((2,))],
        compiler_params=pltpu.CompilerParams(vmem_limit_bytes=1 << 20),
    )(adjoint, gradient)


def solution(mesh):
    return jax.shard_map(
        functools.partial(shards, mesh.shape["gx"], mesh.shape["gy"]),
        mesh=mesh,
        in_specs=(
            P("ha", None, None, ("cand", "gx"), "gy", None),
            P("ha", None, None, ("cand", "gx"), "gy", None),
            P(("cand", "gx"), "gy", None),
            P(),
            P(("cand", "gx"), "gy"),
            P(),
            P(),
        ),
        out_specs=(P("ha", None, None, ("cand", "gx"), "gy", None), P(("cand", "gx"), "gy", None)),
        check_vma=False,
    )
```
